32 devices in a mesh: tm: 8 (over y, x, core), row: 4 (over z).
Axes of the slice: x: 2, y: 2, z: 4, core: 2. Of those that a mesh axis runs over, the one named last changes fastest.
Arguments:
- observations: float32 [64, 128], P('tm'), may hold values from -6 to 6
- sites: int32 [64, 128], P('tm'), may hold values from 0 to 255
- pattern: int32 [64, 8, 3], P('tm'), may hold values from 0 to 7, as said below
- block_values: float32 [64, 8, 3, 128, 128], P('tm', 'row')
- gains: float32 [64, 1024, 128], P('tm', 'row'), may hold values from -0.03 to 0.73
- variances: float32 [64, 128], P('tm'), may hold values from 0.5 to 2
- monotone_bend_strength: float32 [1], replicated, may hold values from 0.2 to 0.9
- initial_mean: float32 [1024], P('row'), may hold values from -6 to 6
Outputs:
- filtered: float32 [64, 1024], P('tm', 'row')
- evidence: float32 [1], replicated
The draws below stay inside these ranges and needn't reach their ends.
Inputs may be any that keep to these rules, and one draw needn't show every extreme that they name: `pattern`: block row r lists r itself first, then two other distinct blocks.
All inputs are finite; a program needn't handle non-finite values.
Results may differ from the reference program's by a relative error of at most 0.0003.
Values sent between devices are 32-bit elements; how exact they have to be, the bound alone decides.
No kernel may reach another device: no remote copies, remote signals or barrier semaphores. Data moves between devices by JAX's collectives and lax.ppermute only.
A program may use at most 128 MiB of HBM per device.

```python
import math
import jax
import jax.numpy as jnp
from jax import lax

POINTS = 256
ORDER = 4
BLOCK = 128
NONZERO = 3
OBS = 128
D = 1024
JUMP_PANELS = 8
HORIZON_SIZE = 64


def shared_sites(key):
    return jax.random.randint(jax.random.fold_in(key, 31), (HORIZON_SIZE, OBS), 0, POINTS).astype(jnp.int32)


def draw_sites(key, part):
    return shared_sites(key)


def draw_gains(key, part):
    observed = shared_sites(key)
    onehot = (observed[:, :, None] == jnp.arange(POINTS, dtype=jnp.int32)[None, None, :]).astype(jnp.float32)
    per_point = jnp.sum(onehot, axis=1)
    repeats = jnp.sum(onehot * per_point[:, None, :], axis=2)
    strength = jax.random.uniform(jax.random.fold_in(key, 32), (HORIZON_SIZE, OBS), jnp.float32, 0.3, 0.7) / repeats
    targets = ORDER * observed
    selector = (jnp.arange(D, dtype=jnp.int32)[None, :, None] == targets[:, None, :]).astype(jnp.float32)
    cross = 0.004
    noise = jnp.clip(jax.random.normal(jax.random.fold_in(key, 34), (HORIZON_SIZE, D, OBS), jnp.float32), -6.0, 6.0) * cross
    return noise + selector * strength[:, None, :]


def draw_pattern(key, part):
    lower = jax.random.randint(jax.random.fold_in(key, 11), (HORIZON_SIZE, JUMP_PANELS, 1), 1, JUMP_PANELS // 2)
    upper = jax.random.randint(jax.random.fold_in(key, 12), (HORIZON_SIZE, JUMP_PANELS, 1), JUMP_PANELS // 2, JUMP_PANELS)
    starts = jnp.zeros((HORIZON_SIZE, JUMP_PANELS, 1), jnp.int32)
    offsets = jnp.concatenate([starts, lower.astype(jnp.int32), upper.astype(jnp.int32)], axis=2)
    block_rows = jnp.arange(JUMP_PANELS, dtype=jnp.int32).reshape(1, JUMP_PANELS, 1)
    return ((block_rows + offsets) % JUMP_PANELS).astype(jnp.int32)


def draw_block_values(key, part):
    low_rate = math.log(1.0 / (4.0 * HORIZON_SIZE))
    high_rate = math.log(1.0 / 30.0)
    rates = jnp.exp(jax.random.uniform(jax.random.fold_in(key, 21), (JUMP_PANELS,), jnp.float32, low_rate, high_rate))
    forgetting_ratio = jnp.exp(-rates)[None, :] * jnp.ones((HORIZON_SIZE, JUMP_PANELS), jnp.float32)
    drawn_spell = jax.random.uniform(jax.random.fold_in(key, 22), (HORIZON_SIZE, JUMP_PANELS), jnp.float32)
    spell_span = jax.random.uniform(jax.random.fold_in(key, 23), (HORIZON_SIZE, JUMP_PANELS), jnp.float32, 0.5, 0.8)
    forgetting_ratio = jnp.where(drawn_spell < 4.0 / HORIZON_SIZE, forgetting_ratio * spell_span, forgetting_ratio)
    spread = 0.1 / math.sqrt(3.0 * BLOCK)
    noise_energy = NONZERO * BLOCK * spread * spread
    noise = jax.random.normal(jax.random.fold_in(key, 25), (HORIZON_SIZE, JUMP_PANELS, NONZERO, BLOCK, BLOCK), jnp.float32) * spread
    kept = jnp.sqrt(jnp.maximum(forgetting_ratio * forgetting_ratio - noise_energy, 0.01))
    identity = jnp.eye(BLOCK, dtype=jnp.float32)
    diagonal = kept[:, :, None, None] * identity[None, None, :, :]
    first = (jnp.arange(NONZERO) == 0).astype(jnp.float32)
    return noise + first[None, None, :, None, None] * diagonal[:, :, None, :, :]


def block_scale(key, shape, cuts, low, high):
    gain, own = 1.0, jax.random.fold_in(key, 6)
    for position, parts in cuts:
        heights = jnp.exp(jax.random.uniform(jax.random.fold_in(own, position), (parts,), jnp.float32, low / len(cuts), high / len(cuts)))
        gain = gain * jnp.repeat(heights, shape[position] // parts).reshape([-1 if axis == position else 1 for axis in range(len(shape))])
    return gain


def gaussian(key, dims, scale, limit, cuts=(), kind=jnp.bfloat16):
    entries = scale * jax.random.normal(key, dims, jnp.float32)
    if cuts:
        entries = entries * block_scale(key, dims, cuts, -0.22, 0.18)
    return jnp.clip(entries, -limit, limit).astype(kind)


def setup_inputs(seed: int = 0) -> dict:
    keys = jax.random.split(jax.random.key(seed), 9)
    return {
        "observations": gaussian(keys[0], (HORIZON_SIZE, OBS), 1.0, 6.0, ((0, 8),), jnp.float32),
        "sites": draw_sites(jax.random.fold_in(keys[8], 71), 0),
        "pattern": draw_pattern(jax.random.fold_in(keys[8], 71), 0),
        "block_values": draw_block_values(jax.random.fold_in(keys[8], 71), 0),
        "gains": draw_gains(jax.random.fold_in(keys[8], 71), 0),
        "variances": jnp.clip(jnp.exp(math.log(2.0) - 1.3862944 * jax.random.uniform(keys[5], (HORIZON_SIZE, OBS), jnp.float32) ** block_scale(keys[5], (HORIZON_SIZE, OBS), ((0, 8),), -0.2, 0.2)), 0.5, 2.0),
        "monotone_bend_strength": jnp.clip(jax.random.uniform(keys[6], (1,), jnp.float32, 0.2, 0.9), 0.2, 0.9),
        "initial_mean": gaussian(keys[7], (D,), 1.0, 6.0, ((0, 4),), jnp.float32),
    }


def reference(observations, sites, pattern, block_values, gains, variances, monotone_bend_strength, initial_mean):
    scale_value = monotone_bend_strength[0]
    bent = jnp.tanh(observations)
    warped_targets = observations + scale_value * bent
    log_jacobian = jnp.log(1.0 + scale_value * (1.0 - bent * bent))

    def advance(current, inputs):
        entry_values, columns, gain_cols, targets, places, spreads = inputs
        blocks = current.reshape(columns.shape[0], -1)
        predicted = jnp.einsum("rjab,rjb->ra", entry_values, blocks[columns], precision=lax.Precision.HIGHEST).reshape(-1)
        innovation = targets - predicted[ORDER * places]
        current = predicted + jnp.dot(gain_cols, innovation, precision=lax.Precision.HIGHEST)
        step_term = jnp.sum(-0.5 * innovation * innovation / spreads - 0.5 * jnp.log(spreads))
        return current, (current, step_term)

    final_mean, outputs = lax.scan(advance, initial_mean, (block_values, pattern, gains, warped_targets, sites, variances))
    filtered, step_terms = outputs
    count = HORIZON_SIZE * OBS
    total = jnp.sum(step_terms) + jnp.sum(log_jacobian) - 0.5 * math.log(2.0 * math.pi) * count
    return filtered, (total / count).reshape(1).astype(jnp.float32)
```

```python
import math

import jax
import jax.numpy as jnp
from jax import lax
from jax.experimental import pallas as pl
from jax.experimental.pallas import tpu as pltpu
from jax.sharding import PartitionSpec as P

ORDER = 4
LANES = 128


def lane_sums(block):
    return jnp.sum(block.T, axis=0, keepdims=True)


def segment_kernel(slots, pattern, places, *refs):
    values, gains = refs[:slots], refs[slots : 2 * slots]
    targets, sites, start, filtered, innovations, mean, predicted = refs[2 * slots :]
    steps, held, nonzero = values[0].shape[:3]
    blocks = start.shape[0]
    mean[...] = start[...]

    def step(t, carry):
        for s in range(slots):
            for h in range(held):
                row = held * places[s] + h
                total = None
                for j in range(nonzero):
                    column = pattern[t, row * nonzero + j]
                    part = values[s][t, h, j] * mean[pl.ds(column, 1), :]
                    total = part if total is None else total + part
                predicted[pl.ds(row, 1), :] = lane_sums(total)
        flat = ORDER * sites[pl.ds(t, 1), :]
        lane = jnp.broadcast_to(flat % LANES, (blocks, LANES))
        picked = jnp.take_along_axis(predicted[...], lane, axis=1)
        block = lax.broadcasted_iota(jnp.int32, (blocks, LANES), 0)
        seen = jnp.sum(jnp.where(block == flat // LANES, picked, 0.0), axis=0, keepdims=True)
        innovation = targets[pl.ds(t, 1), :] - seen
        innovations[pl.ds(t, 1), :] = innovation
        for s in range(slots):
            for h in range(held):
                row = held * places[s] + h
                moved = gains[s][t, pl.ds(h * LANES, LANES), :] * innovation
                updated = predicted[pl.ds(row, 1), :] + lane_sums(moved)
                mean[pl.ds(row, 1), :] = updated
                filtered[t, pl.ds(row, 1), :] = updated
        return carry

    lax.fori_loop(0, steps, step, 0)


def run_segment(pattern, places, values, gains, targets, sites, start):
    slots = len(values)
    steps = values[0].shape[0]
    blocks, lanes = start.shape
    vmem = pl.BlockSpec(memory_space=pltpu.VMEM)
    smem = pl.BlockSpec(memory_space=pltpu.SMEM)

    def body(*refs):
        segment_kernel(slots, *refs)

    return pl.pallas_call(
        body,
        in_specs=[smem, smem] + [vmem] * (2 * slots + 3),
        out_specs=[vmem, vmem],
        out_shape=[
            jax.ShapeDtypeStruct((steps, blocks, lanes), jnp.float32),
            jax.ShapeDtypeStruct((steps, lanes), jnp.float32),
        ],
        scratch_shapes=[
            pltpu.VMEM((blocks, lanes), jnp.float32),
            pltpu.VMEM((blocks, lanes), jnp.float32),
        ],
        compiler_params=pltpu.CompilerParams(vmem_limit_bytes=32 << 20),
        name="segment",
    )(pattern, places, *values, *gains, targets, sites, start)


def on_device(
    observations,
    sites,
    pattern,
    block_values,
    gains,
    variances,
    monotone_bend_strength,
    initial_mean,
):
    segments, rows = lax.axis_size("tm"), lax.axis_size("row")
    tm, row = lax.axis_index("tm"), lax.axis_index("row")
    steps, held = block_values.shape[:2]
    blocks = pattern.shape[1]
    even = tm % 2 == 0

    low = (rows - 1) // 2
    order_even = sorted(range(rows), key=lambda z: (abs(z - low), z))
    order_odd = [rows - 1 - z for z in order_even]

    def order(t):
        return order_even if t % 2 == 0 else order_odd

    def flat(t, z):
        return t * rows + z

    both = ("tm", "row")

    def meet(shard):
        moved = [shard]
        for k in range(1, rows):
            pairs = [(flat(t, order(t)[k]), flat(t, order(t)[0])) for t in range(segments)]
            moved.append(lax.ppermute(shard, both, pairs))
        return moved

    starts = meet(initial_mean.reshape(held, LANES))
    all_values = meet(block_values)
    all_gains = meet(gains)
    places = jnp.where(
        even, jnp.array(order_even, jnp.int32), jnp.array(order_odd, jnp.int32)
    )
    by_even = [starts[order_even.index(z)] for z in range(rows)]
    by_odd = [starts[order_odd.index(z)] for z in range(rows)]
    start = jnp.where(even, jnp.concatenate(by_even), jnp.concatenate(by_odd))

    scale = monotone_bend_strength[0]
    bent = jnp.tanh(observations)
    targets = observations + scale * bent
    log_jacobian = jnp.log(1.0 + scale * (1.0 - bent * bent))
    flat_pattern = pattern.reshape(steps, -1)

    for t in range(segments):
        filtered, innovations = run_segment(
            flat_pattern, places, all_values, all_gains, targets, sites, start
        )
        if t + 1 < segments:
            pair = [(flat(t, order(t)[0]), flat(t + 1, order(t + 1)[0]))]
            arrived = lax.ppermute(filtered[steps - 1], both, pair)
            start = jnp.where(tm == t + 1, arrived, start)

    misfit = jnp.sum(innovations * innovations / variances, axis=0, keepdims=True)

    def parcel(z):
        own_rows = lax.dynamic_slice_in_dim(filtered, held * z, held, 1)
        return jnp.concatenate([own_rows.reshape(steps * held, LANES), misfit])

    is_owner = row == places[0]
    received = jnp.where(is_owner, parcel(places[0]), 0.0)
    for k in range(1, rows):
        pairs = [(flat(t, order(t)[0]), flat(t, order(t)[k])) for t in range(segments)]
        received = received + lax.ppermute(parcel(places[k]), both, pairs)
    own_filtered = received[: steps * held].reshape(steps, held * LANES)
    term = (
        -0.5 * jnp.sum(received[steps * held :])
        + jnp.sum(log_jacobian - 0.5 * jnp.log(variances))
        - 0.5 * math.log(2.0 * math.pi) * observations.size
    )
    total = lax.psum(term, "tm")
    evidence = (total / (observations.size * segments)).reshape(1)
    return own_filtered, evidence


def solution(mesh):
    in_specs = (
        P("tm", None),
        P("tm", None),
        P("tm", None, None),
        P("tm", "row", None, None, None),
        P("tm", "row", None),
        P("tm", None),
        P(),
        P("row"),
    )
    out_specs = (P("tm", "row"), P())
    return jax.shard_map(
        on_device, mesh=mesh, in_specs=in_specs, out_specs=out_specs, check_vma=False
    )
```

```python
import math

import jax
import jax.numpy as jnp
from jax import lax
from jax.experimental import pallas as pl
from jax.experimental.pallas import tpu as pltpu
from jax.sharding import PartitionSpec as P

ORDER = 4
LANES = 128
CHUNKS = (4, 2, 1, 1)
VMEM = pl.BlockSpec(memory_space=pltpu.VMEM)
HBM = pl.BlockSpec(memory_space=pltpu.HBM)
SMEM = pl.BlockSpec(memory_space=pltpu.SMEM)


def split(x):
    high = x.astype(jnp.bfloat16)
    return high, (x - high.astype(jnp.float32)).astype(jnp.bfloat16)


def matmul(a, b):
    return jnp.dot(a, b, preferred_element_type=jnp.float32)


def lane_sums(block):
    return jnp.sum(block.T, axis=0, keepdims=True)


def aligned(row):
    return pl.ds(pl.multiple_of(row * LANES, LANES), LANES)


def compose_kernel(first, last, base, held, nonzero, slots, places, pattern, sites, *refs):
    packs, refs = refs[:slots], refs[slots:]
    targets, refs = refs[0], refs[1:]
    if not first:
        refs = refs[2:]
    high, low, refs = refs[0], refs[1], refs[2:]
    if last:
        whole, refs = refs[0], refs[1:]
    through, seen, store, sems = refs
    width, columns = high.shape
    steps = packs[0].shape[0]
    gain_row = held * nonzero * LANES

    def fetch(s, t):
        return pltpu.make_async_copy(packs[s].at[t], store.at[s, t], sems.at[s, t])

    for t in range(steps):
        for s in range(slots):
            fetch(s, t).start()
    if first:
        rows = lax.broadcasted_iota(jnp.int32, (width, columns), 0)
        cols = lax.broadcasted_iota(jnp.int32, (width, columns), 1)
        high[...] = (rows == cols).astype(jnp.float32).astype(jnp.bfloat16)
        low[...] = jnp.zeros_like(low)

    def step(t, carry):
        for s in range(slots):
            fetch(s, t).wait()
        for s in range(slots):
            for h in range(held):
                row = held * places[s] + h
                picks = [aligned(pattern[base + t, row * nonzero + j]) for j in range(nonzero)]
                parts = [
                    split(store[s, t, pl.ds((h * nonzero + j) * LANES, LANES), :])
                    for j in range(nonzero)
                ]
                up = [p[0] for p in parts]
                down = [p[1] for p in parts]
                tops = [high[pick, :] for pick in picks]
                bottoms = [low[pick, :] for pick in picks]
                through[aligned(row), :] = matmul(
                    jnp.concatenate(up + down + up, axis=1),
                    jnp.concatenate(tops + tops + bottoms),
                )

        def pick_rows(i, carry):
            for u in range(32):
                k = i * 32 + u
                seen[pl.ds(k, 1), :] = through[pl.ds(ORDER * sites[base + t, k], 1), :]
            return carry

        lax.fori_loop(0, LANES // 32, pick_rows, 0)
        target = jnp.broadcast_to(targets[pl.ds(base + t, 1), :], (LANES, LANES)).T
        lane = lax.broadcasted_iota(jnp.int32, (LANES, LANES), 1)
        offset = pl.ds(width, LANES)
        seen[:, offset] = seen[:, offset] - jnp.where(lane == 0, target, 0.0)
        top, bottom = split(seen[...])
        halves = [split(store[s, t, pl.ds(gain_row, held * LANES), :]) for s in range(slots)]
        left = jnp.concatenate([jnp.concatenate([a, b, a], axis=1) for a, b in halves])
        moved = matmul(left, jnp.concatenate([top, top, bottom]))
        for s in range(slots):
            for h in range(held):
                here = aligned(held * places[s] + h)
                at = (s * held + h) * LANES
                new = through[here, :] - moved[at : at + LANES]
                if last:

                    @pl.when(t == steps - 1)
                    def _():
                        whole[here, :] = new

                if not last or steps > 1:
                    a, b = split(new)
                    high[here, :] = a
                    low[here, :] = b
        return carry

    lax.fori_loop(0, steps, step, 0)


def compose(first, last, base, held, nonzero, places, pattern, sites, packs, targets, state):
    slots = len(packs)
    steps = packs[0].shape[0]
    width = slots * held * LANES
    columns = width + LANES
    part = jax.ShapeDtypeStruct((width, columns), jnp.bfloat16)
    out_shape = [part, part]
    if last:
        out_shape.append(jax.ShapeDtypeStruct((width, columns), jnp.float32))

    def body(*refs):
        compose_kernel(first, last, base, held, nonzero, slots, *refs)

    done = pl.pallas_call(
        body,
        in_specs=[SMEM] * 3 + [HBM] * slots + [VMEM] * (1 + len(state)),
        out_specs=[VMEM] * len(out_shape),
        out_shape=out_shape,
        scratch_shapes=[
            pltpu.VMEM((width, columns), jnp.float32),
            pltpu.VMEM((LANES, columns), jnp.float32),
            pltpu.VMEM((slots,) + packs[0].shape, jnp.float32),
            pltpu.SemaphoreType.DMA((slots, steps)),
        ],
        cost_estimate=pl.CostEstimate(
            flops=steps * 2 * width * columns * 3 * (nonzero + 1) * LANES,
            transcendentals=0,
            bytes_accessed=4 * slots * packs[0].size,
        ),
        input_output_aliases={} if first else {slots + 4: 0, slots + 5: 1},
        compiler_params=pltpu.CompilerParams(vmem_limit_bytes=36 << 20),
        name="compose",
    )(places, pattern, sites, *packs, targets, *state)
    return done[2] if last else done


def hop_kernel(whole, start, end):
    blocks = start.shape[0]
    for r in range(blocks):
        rows = pl.ds(r * LANES, LANES)
        total = whole[rows, pl.ds(blocks * LANES, LANES)]
        for c in range(blocks):
            total = total + whole[rows, pl.ds(c * LANES, LANES)] * start[pl.ds(c, 1), :]
        end[pl.ds(r, 1), :] = lane_sums(total)


def hop(whole, start):
    return pl.pallas_call(
        hop_kernel,
        in_specs=[VMEM, VMEM],
        out_specs=VMEM,
        out_shape=jax.ShapeDtypeStruct(start.shape, jnp.float32),
        compiler_params=pltpu.CompilerParams(vmem_limit_bytes=8 << 20),
        name="hop",
    )(whole, start)


def segment_kernel(held, nonzero, slots, chunks, places, pattern, *refs):
    packs = [refs[c * slots : (c + 1) * slots] for c in range(chunks)]
    targets, sites, start, filtered, innovations, mean, predicted = refs[chunks * slots : -2]
    store, sems = refs[-2:]
    steps = store.shape[1]
    blocks = start.shape[0]
    gain_row = held * nonzero * LANES
    t = 0
    for pack in packs:
        for i in range(pack[0].shape[0]):
            for s in range(slots):
                pltpu.make_async_copy(pack[s].at[i], store.at[s, t], sems.at[s, t]).start()
            t += 1
    mean[...] = start[...]

    def step(t, carry):
        for s in range(slots):
            pltpu.make_async_copy(packs[0][s].at[0], store.at[s, t], sems.at[s, t]).wait()
        for s in range(slots):
            for h in range(held):
                row = held * places[s] + h
                total = None
                for j in range(nonzero):
                    column = pattern[t, row * nonzero + j]
                    block = store[s, t, pl.ds((h * nonzero + j) * LANES, LANES), :]
                    part = block * mean[pl.ds(column, 1), :]
                    total = part if total is None else total + part
                predicted[pl.ds(row, 1), :] = lane_sums(total)
        flat = ORDER * sites[pl.ds(t, 1), :]
        lane = jnp.broadcast_to(flat % LANES, (blocks, LANES))
        picked = jnp.take_along_axis(predicted[...], lane, axis=1)
        block = lax.broadcasted_iota(jnp.int32, (blocks, LANES), 0)
        picked = jnp.where(block == flat // LANES, picked, 0.0)
        innovation = targets[pl.ds(t, 1), :] - jnp.sum(picked, axis=0, keepdims=True)
        innovations[pl.ds(t, 1), :] = innovation
        for s in range(slots):
            for h in range(held):
                row = held * places[s] + h
                moved = store[s, t, pl.ds(gain_row + h * LANES, LANES), :] * innovation
                updated = predicted[pl.ds(row, 1), :] + lane_sums(moved)
                mean[pl.ds(row, 1), :] = updated
                filtered[t, pl.ds(row, 1), :] = updated
        return carry

    lax.fori_loop(0, steps, step, 0)


def run_segment(held, nonzero, places, pattern, packs, targets, sites, start):
    chunks, slots = len(packs), len(packs[0])
    steps = targets.shape[0]
    blocks, lanes = start.shape

    def body(*refs):
        segment_kernel(held, nonzero, slots, chunks, *refs)

    return pl.pallas_call(
        body,
        in_specs=[SMEM, SMEM] + [HBM] * (chunks * slots) + [VMEM] * 3,
        out_specs=[VMEM, VMEM],
        out_shape=[
            jax.ShapeDtypeStruct((steps, blocks, lanes), jnp.float32),
            jax.ShapeDtypeStruct((steps, lanes), jnp.float32),
        ],
        scratch_shapes=[
            pltpu.VMEM((blocks, lanes), jnp.float32),
            pltpu.VMEM((blocks, lanes), jnp.float32),
            pltpu.VMEM((slots, steps) + packs[0][0].shape[1:], jnp.float32),
            pltpu.SemaphoreType.DMA((slots, steps)),
        ],
        compiler_params=pltpu.CompilerParams(vmem_limit_bytes=60 << 20),
        name="segment",
    )(places, pattern, *[p for pack in packs for p in pack], targets, sites, start)


def on_device(
    observations,
    sites,
    pattern,
    block_values,
    gains,
    variances,
    monotone_bend_strength,
    initial_mean,
):
    segments, rows = lax.axis_size("tm"), lax.axis_size("row")
    tm, row = lax.axis_index("tm"), lax.axis_index("row")
    steps, held, nonzero = block_values.shape[:3]
    even = tm % 2 == 0

    low = (rows - 1) // 2
    order_even = sorted(range(rows), key=lambda z: (abs(z - low), z))
    order_odd = [rows - 1 - z for z in order_even]

    def order(t):
        return order_even if t % 2 == 0 else order_odd

    def flat(t, z):
        return t * rows + z

    both = ("tm", "row")

    def meet(shard):
        moved = [shard]
        for k in range(1, rows):
            pairs = [(flat(t, order(t)[k]), flat(t, order(t)[0])) for t in range(segments)]
            moved.append(lax.ppermute(shard, both, pairs))
        return moved

    places = jnp.where(
        even, jnp.array(order_even, jnp.int32), jnp.array(order_odd, jnp.int32)
    )
    starts = meet(initial_mean.reshape(held, LANES))
    by_even = [starts[order_even.index(z)] for z in range(rows)]
    by_odd = [starts[order_odd.index(z)] for z in range(rows)]
    start = jnp.where(even, jnp.concatenate(by_even), jnp.concatenate(by_odd))

    scale = monotone_bend_strength[0]
    bent = jnp.tanh(observations)
    targets = observations + scale * bent
    log_jacobian = jnp.log(1.0 + scale * (1.0 - bent * bent))
    flat_pattern = pattern.reshape(steps, -1)

    sizes = CHUNKS if sum(CHUNKS) == steps else (1,) * steps
    packs, base = [], 0
    for size in sizes:
        blocks = block_values[base : base + size].reshape(size, -1, LANES)
        packs.append(meet(jnp.concatenate([blocks, gains[base : base + size]], axis=1)))
        base += size

    state, base = (), 0
    for i, size in enumerate(sizes):
        state = compose(
            i == 0,
            i == len(sizes) - 1,
            base,
            held,
            nonzero,
            places,
            flat_pattern,
            sites,
            packs[i],
            targets,
            state,
        )
        base += size

    mean, begin = start, jnp.where(tm == 0, start, 0.0)
    for t in range(segments - 1):
        pair = [(flat(t, order(t)[0]), flat(t + 1, order(t + 1)[0]))]
        mean = lax.ppermute(hop(state, mean), both, pair)
        begin = begin + mean
    filtered, innovations = run_segment(
        held, nonzero, places, flat_pattern, packs, targets, sites, begin
    )
    misfit = jnp.sum(innovations * innovations / variances, axis=0, keepdims=True)

    def parcel(z):
        own_rows = lax.dynamic_slice_in_dim(filtered, held * z, held, 1)
        return jnp.concatenate([own_rows.reshape(steps * held, LANES), misfit])

    is_owner = row == places[0]
    received = jnp.where(is_owner, parcel(places[0]), 0.0)
    for k in range(1, rows):
        pairs = [(flat(t, order(t)[0]), flat(t, order(t)[k])) for t in range(segments)]
        received = received + lax.ppermute(parcel(places[k]), both, pairs)
    own_filtered = received[: steps * held].reshape(steps, held * LANES)
    term = (
        -0.5 * jnp.sum(received[steps * held :])
        + jnp.sum(log_jacobian - 0.5 * jnp.log(variances))
        - 0.5 * math.log(2.0 * math.pi) * observations.size
    )
    total = lax.psum(term, "tm")
    evidence = (total / (observations.size * segments)).reshape(1)
    return own_filtered, evidence


def solution(mesh):
    in_specs = (
        P("tm", None),
        P("tm", None),
        P("tm", None, None),
        P("tm", "row", None, None, None),
        P("tm", "row", None),
        P("tm", None),
        P(),
        P("row"),
    )
    out_specs = (P("tm", "row"), P())
    return jax.shard_map(
        on_device, mesh=mesh, in_specs=in_specs, out_specs=out_specs, check_vma=False
    )
```

```python
import math

import jax
import jax.numpy as jnp
from jax import lax
from jax.experimental import pallas as pl
from jax.experimental.pallas import tpu as pltpu
from jax.sharding import PartitionSpec as P

ORDER = 4
LANES = 128
CHUNKS = (1, 2, 2, 2, 1)
VMEM = pl.BlockSpec(memory_space=pltpu.VMEM)
UNROLL = 8
HBM = pl.BlockSpec(memory_space=pltpu.HBM)
SMEM = pl.BlockSpec(memory_space=pltpu.SMEM)


def in_hbm(x):
    return pltpu.with_memory_space_constraint(x, pltpu.HBM)


def split(x):
    high = x.astype(jnp.bfloat16)
    return high, (x - high.astype(jnp.float32)).astype(jnp.bfloat16)


def matmul(a, b):
    return jnp.dot(a, b, preferred_element_type=jnp.float32)


def lane_sums(block):
    return jnp.sum(block.T, axis=0, keepdims=True)


def aligned(row):
    return pl.ds(pl.multiple_of(row * LANES, LANES), LANES)


def compose_kernel(first, last, base, steps, held, nonzero, slots, places, pattern, sites, *refs):
    packs, refs = refs[:slots], refs[slots:]
    targets, refs = refs[0], refs[1:]
    if not first:
        refs = refs[2:]
    high, low, refs = refs[0], refs[1], refs[2:]
    if last:
        whole, refs = refs[0], refs[1:]
    through, seen, store, sems = refs
    width, columns = high.shape
    pack_rows = store.shape[2]
    gain_row = held * nonzero * LANES

    def fetch(s, t):
        rows = pl.ds(t * pack_rows, pack_rows)
        return pltpu.make_async_copy(packs[s].at[rows, :], store.at[s, t], sems.at[s, t])

    for t in range(steps):
        for s in range(slots):
            fetch(s, t).start()
    if first:
        rows = lax.broadcasted_iota(jnp.int32, (width, columns), 0)
        cols = lax.broadcasted_iota(jnp.int32, (width, columns), 1)
        high[...] = (rows == cols).astype(jnp.float32).astype(jnp.bfloat16)
        low[...] = jnp.zeros_like(low)

    def step(t, carry):
        for s in range(slots):
            fetch(s, t).wait()

        def block_row(i, carry):
            s, h = i // held, i % held
            row = held * places[s] + h
            picks = [aligned(pattern[base + t, row * nonzero + j]) for j in range(nonzero)]
            parts = [split(store[s, t, aligned(h * nonzero + j), :]) for j in range(nonzero)]
            up = [p[0] for p in parts]
            down = [p[1] for p in parts]
            tops = [high[pick, :] for pick in picks]
            bottoms = [low[pick, :] for pick in picks]
            through[aligned(row), :] = matmul(
                jnp.concatenate(up + down + up, axis=1),
                jnp.concatenate(tops + tops + bottoms),
            )
            return carry

        lax.fori_loop(0, slots * held, block_row, 0, unroll=UNROLL)

        def pick_rows(i, carry):
            for u in range(32):
                k = i * 32 + u
                seen[pl.ds(k, 1), :] = through[pl.ds(ORDER * sites[base + t, k], 1), :]
            return carry

        lax.fori_loop(0, LANES // 32, pick_rows, 0)
        target = jnp.broadcast_to(targets[pl.ds(base + t, 1), :], (LANES, LANES)).T
        lane = lax.broadcasted_iota(jnp.int32, (LANES, LANES), 1)
        offset = pl.ds(width, LANES)
        seen[:, offset] = seen[:, offset] - jnp.where(lane == 0, target, 0.0)
        top, bottom = split(seen[...])
        halves = [split(store[s, t, pl.ds(gain_row, held * LANES), :]) for s in range(slots)]
        left = jnp.concatenate([jnp.concatenate([a, b, a], axis=1) for a, b in halves])
        moved = matmul(left, jnp.concatenate([top, top, bottom]))
        for s in range(slots):
            for h in range(held):
                here = aligned(held * places[s] + h)
                at = (s * held + h) * LANES
                new = through[here, :] - moved[at : at + LANES]
                if last:

                    @pl.when(t == steps - 1)
                    def _(here=here, new=new):
                        whole[here, :] = new

                if not last or steps > 1:
                    a, b = split(new)
                    high[here, :] = a
                    low[here, :] = b
        return carry

    lax.fori_loop(0, steps, step, 0)


def compose(first, last, base, steps, held, nonzero, places, pattern, sites, packs, targets, state):
    slots = len(packs)
    pack_rows = held * (nonzero + 1) * LANES
    width = slots * held * LANES
    columns = width + LANES
    part = jax.ShapeDtypeStruct((width, columns), jnp.bfloat16)
    out_shape = [part, part]
    if last:
        out_shape.append(jax.ShapeDtypeStruct((width, columns), jnp.float32))

    def body(*refs):
        compose_kernel(first, last, base, steps, held, nonzero, slots, *refs)

    done = pl.pallas_call(
        body,
        in_specs=[SMEM] * 3 + [HBM] * slots + [VMEM] * (1 + len(state)),
        out_specs=[VMEM] * len(out_shape),
        out_shape=out_shape,
        scratch_shapes=[
            pltpu.VMEM((width, columns), jnp.float32),
            pltpu.VMEM((LANES, columns), jnp.float32),
            pltpu.VMEM((slots, steps, pack_rows, LANES), jnp.float32),
            pltpu.SemaphoreType.DMA((slots, steps)),
        ],
        cost_estimate=pl.CostEstimate(
            flops=steps * 2 * width * columns * 3 * (nonzero + 1) * LANES,
            transcendentals=0,
            bytes_accessed=4 * slots * steps * pack_rows * LANES,
        ),
        input_output_aliases={} if first else {slots + 4: 0, slots + 5: 1},
        compiler_params=pltpu.CompilerParams(vmem_limit_bytes=36 << 20),
        name="compose",
    )(places, pattern, sites, *[in_hbm(p) for p in packs], targets, *state)
    return done[2] if last else done


def hop_kernel(whole, start, end):
    blocks = start.shape[0]
    for r in range(blocks):
        rows = pl.ds(r * LANES, LANES)
        total = whole[rows, pl.ds(blocks * LANES, LANES)]
        for c in range(blocks):
            total = total + whole[rows, pl.ds(c * LANES, LANES)] * start[pl.ds(c, 1), :]
        end[pl.ds(r, 1), :] = lane_sums(total)


def hop(whole, start):
    return pl.pallas_call(
        hop_kernel,
        in_specs=[VMEM, VMEM],
        out_specs=VMEM,
        out_shape=jax.ShapeDtypeStruct(start.shape, jnp.float32),
        compiler_params=pltpu.CompilerParams(vmem_limit_bytes=8 << 20),
        name="hop",
    )(whole, start)


def stage_kernel(slots, sizes, *refs):
    packs, store, sems = refs[: slots * len(sizes)], refs[-2], refs[-1]
    rows = store.shape[2]
    copies, t = [], 0
    for c, size in enumerate(sizes):
        for i in range(size):
            for s in range(slots):
                copies.append(
                    pltpu.make_async_copy(
                        packs[c * slots + s].at[pl.ds(i * rows, rows), :],
                        store.at[s, t],
                        sems.at[s, t],
                    )
                )
            t += 1
    for copy in copies:
        copy.start()
    for copy in copies:
        copy.wait()


def stage(sizes, pack_rows, packs, after):
    slots, steps = len(packs[0]), sum(sizes)

    def body(*refs):
        stage_kernel(slots, sizes, *refs)

    shape = (slots, steps, pack_rows, LANES)
    return pl.pallas_call(
        body,
        in_specs=[HBM] * (slots * len(sizes)) + [VMEM],
        out_specs=VMEM,
        out_shape=jax.ShapeDtypeStruct(shape, jnp.float32),
        scratch_shapes=[pltpu.SemaphoreType.DMA((slots, steps))],
        cost_estimate=pl.CostEstimate(
            flops=0, transcendentals=0, bytes_accessed=8 * math.prod(shape)
        ),
        compiler_params=pltpu.CompilerParams(vmem_limit_bytes=24 << 20),
        name="stage",
    )(*[in_hbm(p) for pack in packs for p in pack], after)


def segment_kernel(held, nonzero, places, pattern, owner, store, *refs):
    targets, sites, weights, start, parcels, mean, predicted = refs
    slots, steps = store.shape[:2]
    blocks = start.shape[0]
    gain_row = held * nonzero * LANES
    mean[...] = start[...]
    mine = owner[0] == 1

    def step(t, misfit):
        for s in range(slots):
            for h in range(held):
                row = held * places[s] + h
                total = None
                for j in range(nonzero):
                    column = pattern[t, row * nonzero + j]
                    block = store[s, t, pl.ds((h * nonzero + j) * LANES, LANES), :]
                    part = block * mean[pl.ds(column, 1), :]
                    total = part if total is None else total + part
                predicted[pl.ds(row, 1), :] = lane_sums(total)
        flat = ORDER * sites[pl.ds(t, 1), :]
        lane = jnp.broadcast_to(flat % LANES, (blocks, LANES))
        picked = jnp.take_along_axis(predicted[...], lane, axis=1)
        block = lax.broadcasted_iota(jnp.int32, (blocks, LANES), 0)
        picked = jnp.where(block == flat // LANES, picked, 0.0)
        innovation = targets[pl.ds(t, 1), :] - jnp.sum(picked, axis=0, keepdims=True)
        for s in range(slots):
            for h in range(held):
                row = held * places[s] + h
                moved = store[s, t, pl.ds(gain_row + h * LANES, LANES), :] * innovation
                updated = predicted[pl.ds(row, 1), :] + lane_sums(moved)
                mean[pl.ds(row, 1), :] = updated
                parcels[s, pl.ds(t * held + h, 1), :] = jnp.where(mine, updated, 0.0)
        return misfit + innovation * innovation * weights[pl.ds(t, 1), :]

    misfit = lax.fori_loop(0, steps, step, jnp.zeros((1, LANES), jnp.float32))
    for s in range(slots):
        parcels[s, pl.ds(steps * held, 1), :] = jnp.where(mine, misfit, 0.0)


def run_segment(held, nonzero, places, pattern, owner, store, targets, sites, weights, start):
    slots, steps = store.shape[:2]

    def body(*refs):
        segment_kernel(held, nonzero, *refs)

    return pl.pallas_call(
        body,
        in_specs=[SMEM] * 3 + [VMEM] * 5,
        out_specs=VMEM,
        out_shape=jax.ShapeDtypeStruct((slots, steps * held + 1, LANES), jnp.float32),
        scratch_shapes=[
            pltpu.VMEM(start.shape, jnp.float32),
            pltpu.VMEM(start.shape, jnp.float32),
        ],
        compiler_params=pltpu.CompilerParams(vmem_limit_bytes=24 << 20),
        name="segment",
    )(places, pattern, owner, store, targets, sites, weights, start)


def on_device(
    observations,
    sites,
    pattern,
    block_values,
    gains,
    variances,
    monotone_bend_strength,
    initial_mean,
):
    segments, rows = lax.axis_size("tm"), lax.axis_size("row")
    tm, row = lax.axis_index("tm"), lax.axis_index("row")
    steps, held, nonzero = block_values.shape[:3]
    even = tm % 2 == 0

    low = (rows - 1) // 2
    order_even = sorted(range(rows), key=lambda z: (abs(z - low), z))
    order_odd = [rows - 1 - z for z in order_even]

    def order(t):
        return order_even if t % 2 == 0 else order_odd

    def flat(t, z):
        return t * rows + z

    both = ("tm", "row")

    def meet(shard):
        moved = [shard]
        for k in range(1, rows):
            pairs = [(flat(t, order(t)[k]), flat(t, order(t)[0])) for t in range(segments)]
            moved.append(lax.ppermute(shard, both, pairs))
        return moved

    places = jnp.where(
        even, jnp.array(order_even, jnp.int32), jnp.array(order_odd, jnp.int32)
    )
    scale = monotone_bend_strength[0]
    bent = jnp.tanh(observations)
    targets = observations + scale * bent
    log_jacobian = jnp.log(1.0 + scale * (1.0 - bent * bent))
    flat_pattern = pattern.reshape(steps, -1)

    sizes = CHUNKS if sum(CHUNKS) == steps else (1,) * steps
    pack_rows = held * (nonzero + 1) * LANES
    packs, base = [], 0
    for i, size in enumerate(sizes):
        blocks = block_values[base : base + size].reshape(size, -1, LANES)
        pack = jnp.concatenate([blocks, gains[base : base + size]], axis=1)
        pack = pack.reshape(size * pack_rows, LANES)
        if i == 0:
            first = initial_mean.reshape(held, LANES)
            pack = jnp.concatenate([pack, jnp.pad(first, ((0, -held % 8), (0, 0)))])
        packs.append(meet(pack))
        base += size

    starts = [p[sizes[0] * pack_rows :][:held] for p in packs[0]]
    by_even = [starts[order_even.index(z)] for z in range(rows)]
    by_odd = [starts[order_odd.index(z)] for z in range(rows)]
    start = jnp.where(even, jnp.concatenate(by_even), jnp.concatenate(by_odd))

    state, base = (), 0
    for i, size in enumerate(sizes):
        state = compose(
            i == 0,
            i == len(sizes) - 1,
            base,
            size,
            held,
            nonzero,
            places,
            flat_pattern,
            sites,
            packs[i],
            targets,
            state,
        )
        base += size

    mean, begin = start, jnp.where(tm == 0, start, 0.0)
    for t in range(segments - 1):
        pair = [(flat(t, order(t)[0]), flat(t + 1, order(t + 1)[0]))]
        ended = hop(state, mean)
        mean = lax.ppermute(ended, both, pair)
        begin = begin + mean
    store = stage(sizes, pack_rows, packs, ended)
    owner = (row == places[:1]).astype(jnp.int32)
    local = run_segment(
        held,
        nonzero,
        places,
        flat_pattern,
        owner,
        store,
        targets,
        sites,
        1.0 / variances,
        begin,
    )

    while local.shape[0] > 1:
        half = local.shape[0] // 2
        pairs = [
            (flat(t, order(t)[i]), flat(t, order(t)[i + half]))
            for t in range(segments)
            for i in range(0, rows, 2 * half)
        ]
        local = local[:half] + lax.ppermute(local[half:], both, pairs)
    own_filtered = local[0, : steps * held].reshape(steps, held * LANES)

    term = jnp.sum(log_jacobian - 0.5 * jnp.log(variances), axis=0, keepdims=True)
    term = term - 0.5 * local[0, steps * held :]
    if segments & (segments - 1):
        term = lax.psum(term, "tm")
    else:
        reach = 1
        while reach < segments:
            term = term + lax.ppermute(term, "tm", [(t, t ^ reach) for t in range(segments)])
            reach *= 2
    count = observations.size * segments
    evidence = jnp.sum(term) / count - 0.5 * math.log(2.0 * math.pi)
    return own_filtered, evidence.reshape(1)


def solution(mesh):
    in_specs = (
        P("tm", None),
        P("tm", None),
        P("tm", None, None),
        P("tm", "row", None, None, None),
        P("tm", "row", None),
        P("tm", None),
        P(),
        P("row"),
    )
    out_specs = (P("tm", "row"), P())
    return jax.shard_map(
        on_device, mesh=mesh, in_specs=in_specs, out_specs=out_specs, check_vma=False
    )
```

```python
import math

import jax
import jax.numpy as jnp
from jax import lax
from jax.experimental import pallas as pl
from jax.experimental.pallas import tpu as pltpu
from jax.sharding import PartitionSpec as P

ORDER = 4
LANES = 128
CHUNKS = (1, 2, 2, 2, 1)
VMEM = pl.BlockSpec(memory_space=pltpu.VMEM)
UNROLL = 8
HBM = pl.BlockSpec(memory_space=pltpu.HBM)
SMEM = pl.BlockSpec(memory_space=pltpu.SMEM)


def in_hbm(x):
    return pltpu.with_memory_space_constraint(x, pltpu.HBM)


def split(x):
    high = x.astype(jnp.bfloat16)
    return high, (x - high.astype(jnp.float32)).astype(jnp.bfloat16)


def matmul(a, b):
    return jnp.dot(a, b, preferred_element_type=jnp.float32)


def lane_sums(block):
    return jnp.sum(block.T, axis=0, keepdims=True)


def aligned(row):
    return pl.ds(pl.multiple_of(row * LANES, LANES), LANES)


def compose_kernel(first, last, base, steps, held, nonzero, slots, places, pattern, sites, *refs):
    packs, refs = refs[:slots], refs[slots:]
    targets, refs = refs[0], refs[1:]
    if not first:
        refs = refs[2:]
    high, low, refs = refs[0], refs[1], refs[2:]
    if last:
        whole, refs = refs[0], refs[1:]
    through, seen, store, sems = refs
    width, columns = high.shape
    pack_rows = store.shape[2]
    gain_row = held * nonzero * LANES

    def fetch(s, t):
        rows = pl.ds(t * pack_rows, pack_rows)
        return pltpu.make_async_copy(packs[s].at[rows, :], store.at[s, t], sems.at[s, t])

    for t in range(steps):
        for s in range(slots):
            fetch(s, t).start()
    if first:
        rows = lax.broadcasted_iota(jnp.int32, (width, columns), 0)
        cols = lax.broadcasted_iota(jnp.int32, (width, columns), 1)
        high[...] = (rows == cols).astype(jnp.float32).astype(jnp.bfloat16)
        low[...] = jnp.zeros_like(low)

    def step(t, carry):
        for s in range(slots):
            fetch(s, t).wait()

        def block_row(i, carry):
            s, h = i // held, i % held
            row = held * places[s] + h
            picks = [aligned(pattern[base + t, row * nonzero + j]) for j in range(nonzero)]
            parts = [split(store[s, t, aligned(h * nonzero + j), :]) for j in range(nonzero)]
            up = [p[0] for p in parts]
            down = [p[1] for p in parts]
            tops = [high[pick, :] for pick in picks]
            bottoms = [low[pick, :] for pick in picks]
            through[aligned(row), :] = matmul(
                jnp.concatenate(up + down + up, axis=1),
                jnp.concatenate(tops + tops + bottoms),
            )
            return carry

        lax.fori_loop(0, slots * held, block_row, 0, unroll=UNROLL)

        def pick_rows(i, carry):
            for u in range(32):
                k = i * 32 + u
                seen[pl.ds(k, 1), :] = through[pl.ds(ORDER * sites[base + t, k], 1), :]
            return carry

        lax.fori_loop(0, LANES // 32, pick_rows, 0)
        target = jnp.broadcast_to(targets[pl.ds(base + t, 1), :], (LANES, LANES)).T
        lane = lax.broadcasted_iota(jnp.int32, (LANES, LANES), 1)
        offset = pl.ds(width, LANES)
        seen[:, offset] = seen[:, offset] - jnp.where(lane == 0, target, 0.0)
        top, bottom = split(seen[...])
        halves = [split(store[s, t, pl.ds(gain_row, held * LANES), :]) for s in range(slots)]
        left = jnp.concatenate([jnp.concatenate([a, b, a], axis=1) for a, b in halves])
        moved = matmul(left, jnp.concatenate([top, top, bottom]))
        for s in range(slots):
            for h in range(held):
                here = aligned(held * places[s] + h)
                at = (s * held + h) * LANES
                new = through[here, :] - moved[at : at + LANES]
                if last:

                    @pl.when(t == steps - 1)
                    def _(here=here, new=new):
                        whole[here, :] = new

                if not last or steps > 1:
                    a, b = split(new)
                    high[here, :] = a
                    low[here, :] = b
        return carry

    lax.fori_loop(0, steps, step, 0)


def compose(first, last, base, steps, held, nonzero, places, pattern, sites, packs, targets, state):
    slots = len(packs)
    pack_rows = held * (nonzero + 1) * LANES
    width = slots * held * LANES
    columns = width + LANES
    part = jax.ShapeDtypeStruct((width, columns), jnp.bfloat16)
    out_shape = [part, part]
    if last:
        out_shape.append(jax.ShapeDtypeStruct((width, columns), jnp.float32))

    def body(*refs):
        compose_kernel(first, last, base, steps, held, nonzero, slots, *refs)

    done = pl.pallas_call(
        body,
        in_specs=[SMEM] * 3 + [HBM] * slots + [VMEM] * (1 + len(state)),
        out_specs=[VMEM] * len(out_shape),
        out_shape=out_shape,
        scratch_shapes=[
            pltpu.VMEM((width, columns), jnp.float32),
            pltpu.VMEM((LANES, columns), jnp.float32),
            pltpu.VMEM((slots, steps, pack_rows, LANES), jnp.float32),
            pltpu.SemaphoreType.DMA((slots, steps)),
        ],
        cost_estimate=pl.CostEstimate(
            flops=steps * 2 * width * columns * 3 * (nonzero + 1) * LANES,
            transcendentals=0,
            bytes_accessed=4 * slots * steps * pack_rows * LANES,
        ),
        input_output_aliases={} if first else {slots + 4: 0, slots + 5: 1},
        compiler_params=pltpu.CompilerParams(vmem_limit_bytes=36 << 20),
        name="compose",
    )(places, pattern, sites, *[in_hbm(p) for p in packs], targets, *state)
    return done[2] if last else done


def hop_kernel(whole, start, end):
    blocks = start.shape[0]
    for r in range(blocks):
        rows = pl.ds(r * LANES, LANES)
        total = whole[rows, pl.ds(blocks * LANES, LANES)]
        for c in range(blocks):
            total = total + whole[rows, pl.ds(c * LANES, LANES)] * start[pl.ds(c, 1), :]
        end[pl.ds(r, 1), :] = lane_sums(total)


def hop(whole, start):
    return pl.pallas_call(
        hop_kernel,
        in_specs=[VMEM, VMEM],
        out_specs=VMEM,
        out_shape=jax.ShapeDtypeStruct(start.shape, jnp.float32),
        compiler_params=pltpu.CompilerParams(vmem_limit_bytes=8 << 20),
        name="hop",
    )(whole, start)


def stage_kernel(slots, sizes, *refs):
    packs, store, sems = refs[: slots * len(sizes)], refs[-2], refs[-1]
    rows = store.shape[2]
    copies, t = [], 0
    for c, size in enumerate(sizes):
        for i in range(size):
            for s in range(slots):
                copies.append(
                    pltpu.make_async_copy(
                        packs[c * slots + s].at[pl.ds(i * rows, rows), :],
                        store.at[s, t],
                        sems.at[s, t],
                    )
                )
            t += 1
    for copy in copies:
        copy.start()
    for copy in copies:
        copy.wait()


def stage(sizes, pack_rows, packs, after):
    slots, steps = len(packs[0]), sum(sizes)

    def body(*refs):
        stage_kernel(slots, sizes, *refs)

    shape = (slots, steps, pack_rows, LANES)
    return pl.pallas_call(
        body,
        in_specs=[HBM] * (slots * len(sizes)) + [VMEM],
        out_specs=VMEM,
        out_shape=jax.ShapeDtypeStruct(shape, jnp.float32),
        scratch_shapes=[pltpu.SemaphoreType.DMA((slots, steps))],
        cost_estimate=pl.CostEstimate(
            flops=0, transcendentals=0, bytes_accessed=8 * math.prod(shape)
        ),
        compiler_params=pltpu.CompilerParams(vmem_limit_bytes=24 << 20),
        name="stage",
    )(*[in_hbm(p) for pack in packs for p in pack], after)


def segment_kernel(held, nonzero, places, pattern, owner, store, *refs):
    targets, sites, weights, start, parcels, mean, predicted = refs
    slots, steps = store.shape[:2]
    blocks = start.shape[0]
    gain_row = held * nonzero * LANES
    mean[...] = start[...]
    mine = owner[0] == 1

    def step(t, misfit):
        for s in range(slots):
            for h in range(held):
                row = held * places[s] + h
                total = None
                for j in range(nonzero):
                    column = pattern[t, row * nonzero + j]
                    block = store[s, t, pl.ds((h * nonzero + j) * LANES, LANES), :]
                    part = block * mean[pl.ds(column, 1), :]
                    total = part if total is None else total + part
                predicted[pl.ds(row, 1), :] = lane_sums(total)
        flat = ORDER * sites[pl.ds(t, 1), :]
        lane = jnp.broadcast_to(flat % LANES, (blocks, LANES))
        picked = jnp.take_along_axis(predicted[...], lane, axis=1)
        block = lax.broadcasted_iota(jnp.int32, (blocks, LANES), 0)
        picked = jnp.where(block == flat // LANES, picked, 0.0)
        innovation = targets[pl.ds(t, 1), :] - jnp.sum(picked, axis=0, keepdims=True)
        for s in range(slots):
            for h in range(held):
                row = held * places[s] + h
                moved = store[s, t, pl.ds(gain_row + h * LANES, LANES), :] * innovation
                updated = predicted[pl.ds(row, 1), :] + lane_sums(moved)
                mean[pl.ds(row, 1), :] = updated
                parcels[s, pl.ds(t * held + h, 1), :] = jnp.where(mine, updated, 0.0)
        return misfit + innovation * innovation * weights[pl.ds(t, 1), :]

    misfit = lax.fori_loop(0, steps, step, jnp.zeros((1, LANES), jnp.float32))
    for s in range(slots):
        parcels[s, pl.ds(steps * held, 1), :] = jnp.where(mine, misfit, 0.0)


def run_segment(held, nonzero, places, pattern, owner, store, targets, sites, weights, start):
    slots, steps = store.shape[:2]

    def body(*refs):
        segment_kernel(held, nonzero, *refs)

    return pl.pallas_call(
        body,
        in_specs=[SMEM] * 3 + [VMEM] * 5,
        out_specs=VMEM,
        out_shape=jax.ShapeDtypeStruct((slots, steps * held + 1, LANES), jnp.float32),
        scratch_shapes=[
            pltpu.VMEM(start.shape, jnp.float32),
            pltpu.VMEM(start.shape, jnp.float32),
        ],
        compiler_params=pltpu.CompilerParams(vmem_limit_bytes=24 << 20),
        name="segment",
    )(places, pattern, owner, store, targets, sites, weights, start)


def on_device(
    observations,
    sites,
    pattern,
    block_values,
    gains,
    variances,
    monotone_bend_strength,
    initial_mean,
):
    segments, rows = lax.axis_size("tm"), lax.axis_size("row")
    tm, row = lax.axis_index("tm"), lax.axis_index("row")
    steps, held, nonzero = block_values.shape[:3]
    even = tm % 2 == 0

    low = (rows - 1) // 2
    order_even = sorted(range(rows), key=lambda z: (abs(z - low), z))
    order_odd = [rows - 1 - z for z in order_even]

    def order(t):
        return order_even if t % 2 == 0 else order_odd

    def flat(t, z):
        return t * rows + z

    both = ("tm", "row")

    def meet(shard):
        moved = [shard]
        for k in range(1, rows):
            pairs = [(flat(t, order(t)[k]), flat(t, order(t)[0])) for t in range(segments)]
            moved.append(lax.ppermute(shard, both, pairs))
        return moved

    places = jnp.where(
        even, jnp.array(order_even, jnp.int32), jnp.array(order_odd, jnp.int32)
    )
    scale = monotone_bend_strength[0]
    bent = jnp.tanh(observations)
    targets = observations + scale * bent
    log_jacobian = jnp.log(1.0 + scale * (1.0 - bent * bent))
    flat_pattern = pattern.reshape(steps, -1)

    sizes = CHUNKS if sum(CHUNKS) == steps else (1,) * steps
    pack_rows = held * (nonzero + 1) * LANES
    packs, base = [], 0
    for i, size in enumerate(sizes):
        blocks = block_values[base : base + size].reshape(size, -1, LANES)
        pack = jnp.concatenate([blocks, gains[base : base + size]], axis=1)
        pack = pack.reshape(size * pack_rows, LANES)
        if i == 0:
            first = initial_mean.reshape(held, LANES)
            pack = jnp.concatenate([pack, jnp.pad(first, ((0, -held % 8), (0, 0)))])
        packs.append(pack)
        base += size

    packs[:2] = [meet(pack) for pack in packs[:2]]
    state, base = (), 0
    for i, size in enumerate(sizes):
        state = compose(
            i == 0,
            i == len(sizes) - 1,
            base,
            size,
            held,
            nonzero,
            places,
            flat_pattern,
            sites,
            packs[i],
            targets,
            state,
        )
        base += size
        if i + 2 < len(sizes):
            packs[i + 2], *state = lax.optimization_barrier((packs[i + 2], *state))
            packs[i + 2] = meet(packs[i + 2])

    starts = [p[sizes[0] * pack_rows :][:held] for p in packs[0]]
    by_even = [starts[order_even.index(z)] for z in range(rows)]
    by_odd = [starts[order_odd.index(z)] for z in range(rows)]
    start = jnp.where(even, jnp.concatenate(by_even), jnp.concatenate(by_odd))

    mean, begin = start, jnp.where(tm == 0, start, 0.0)
    for t in range(segments - 1):
        pair = [(flat(t, order(t)[0]), flat(t + 1, order(t + 1)[0]))]
        ended = hop(state, mean)
        mean = lax.ppermute(ended, both, pair)
        begin = begin + mean
        if t == min(2, segments - 2):
            store = stage(sizes, pack_rows, packs, ended)
    owner = (row == places[:1]).astype(jnp.int32)
    local = run_segment(
        held,
        nonzero,
        places,
        flat_pattern,
        owner,
        store,
        targets,
        sites,
        1.0 / variances,
        begin,
    )

    while local.shape[0] > 1:
        half = local.shape[0] // 2
        pairs = [
            (flat(t, order(t)[i]), flat(t, order(t)[i + half]))
            for t in range(segments)
            for i in range(0, rows, 2 * half)
        ]
        local = local[:half] + lax.ppermute(local[half:], both, pairs)
    own_filtered = local[0, : steps * held].reshape(steps, held * LANES)

    term = jnp.sum(log_jacobian - 0.5 * jnp.log(variances), axis=0, keepdims=True)
    term = term - 0.5 * local[0, steps * held :]
    if segments & (segments - 1):
        term = lax.psum(term, "tm")
    else:
        reach = 1
        while reach < segments:
            term = term + lax.ppermute(term, "tm", [(t, t ^ reach) for t in range(segments)])
            reach *= 2
    count = observations.size * segments
    evidence = jnp.sum(term) / count - 0.5 * math.log(2.0 * math.pi)
    return own_filtered, evidence.reshape(1)


def solution(mesh):
    in_specs = (
        P("tm", None),
        P("tm", None),
        P("tm", None, None),
        P("tm", "row", None, None, None),
        P("tm", "row", None),
        P("tm", None),
        P(),
        P("row"),
    )
    out_specs = (P("tm", "row"), P())
    return jax.shard_map(
        on_device, mesh=mesh, in_specs=in_specs, out_specs=out_specs, check_vma=False
    )
```

```python
import math

import jax
import jax.numpy as jnp
from jax import lax
from jax.experimental import pallas as pl
from jax.experimental.pallas import tpu as pltpu
from jax.sharding import PartitionSpec as P

ORDER = 4
LANES = 128
CHUNKS = (1, 2, 2, 2, 1)
STAGED = 2
VMEM = pl.BlockSpec(memory_space=pltpu.VMEM)
HBM = pl.BlockSpec(memory_space=pltpu.HBM)
SMEM = pl.BlockSpec(memory_space=pltpu.SMEM)


def in_hbm(x):
    return pltpu.with_memory_space_constraint(x, pltpu.HBM)


def split(x):
    high = x.astype(jnp.bfloat16)
    return high, (x - high.astype(jnp.float32)).astype(jnp.bfloat16)


def matmul(a, b):
    return jnp.dot(a, b, preferred_element_type=jnp.float32)


def lane_sums(block):
    return jnp.sum(block.T, axis=0, keepdims=True)


def aligned(row):
    return pl.ds(pl.multiple_of(row * LANES, LANES), LANES)


def compose_kernel(first, last, base, steps, held, nonzero, slots, places, pattern, sites, *refs):
    packs, refs = refs[:slots], refs[slots:]
    targets, refs = refs[0], refs[1:]
    if not first:
        refs = refs[2:]
    high, low, refs = refs[0], refs[1], refs[2:]
    if last:
        whole, refs = refs[0], refs[1:]
    through, seen, refs = refs[0], refs[1], refs[2:]
    if not last:
        store, sems = refs
    width, columns = high.shape
    pack_rows = held * (nonzero + 1) * LANES
    gain_row = held * nonzero * LANES

    def fetch(s, t):
        rows = pl.ds(t * pack_rows, pack_rows)
        return pltpu.make_async_copy(packs[s].at[rows, :], store.at[s, t], sems.at[s, t])

    def load(s, t, at):
        if last:
            return packs[s][pl.ds(t * pack_rows + at.start, at.size), :]
        return store[s, t, at, :]

    if not last:
        for t in range(steps):
            for s in range(slots):
                fetch(s, t).start()
    def step(t, carry):
        if not last:
            for s in range(slots):
                fetch(s, t).wait()

        def block_row(s, h):
            row = held * places[s] + h
            picks = [aligned(pattern[base + t, row * nonzero + j]) for j in range(nonzero)]
            if first:
                for j in range(nonzero):
                    block = load(s, t, aligned(h * nonzero + j))
                    through[aligned(row), picks[j]] = through[aligned(row), picks[j]] + block
                return
            parts = [split(load(s, t, aligned(h * nonzero + j))) for j in range(nonzero)]
            up = [p[0] for p in parts]
            down = [p[1] for p in parts]
            tops = [high[pick, :] for pick in picks]
            bottoms = [low[pick, :] for pick in picks]
            through[aligned(row), :] = matmul(
                jnp.concatenate(up + down + up, axis=1),
                jnp.concatenate(tops + tops + bottoms),
            )

        if first:
            through[...] = jnp.zeros_like(through)
        for s in range(slots):
            for h in range(held):
                block_row(s, h)

        def pick_rows(i, carry):
            for u in range(32):
                k = i * 32 + u
                seen[pl.ds(k, 1), :] = through[pl.ds(ORDER * sites[base + t, k], 1), :]
            return carry

        lax.fori_loop(0, LANES // 32, pick_rows, 0)
        target = jnp.broadcast_to(targets[pl.ds(base + t, 1), :], (LANES, LANES)).T
        lane = lax.broadcasted_iota(jnp.int32, (LANES, LANES), 1)
        offset = pl.ds(width, LANES)
        seen[:, offset] = seen[:, offset] - jnp.where(lane == 0, target, 0.0)
        top, bottom = split(seen[...])
        halves = [split(load(s, t, pl.ds(gain_row, held * LANES))) for s in range(slots)]
        left = jnp.concatenate([jnp.concatenate([a, b, a], axis=1) for a, b in halves])
        moved = matmul(left, jnp.concatenate([top, top, bottom]))
        for s in range(slots):
            for h in range(held):
                here = aligned(held * places[s] + h)
                at = (s * held + h) * LANES
                new = through[here, :] - moved[at : at + LANES]
                if last:

                    @pl.when(t == steps - 1)
                    def _(here=here, new=new):
                        whole[here, :] = new

                if not last or steps > 1:
                    a, b = split(new)
                    high[here, :] = a
                    low[here, :] = b
        return carry

    lax.fori_loop(0, steps, step, 0)


def compose(first, last, base, steps, held, nonzero, places, pattern, sites, packs, targets, state):
    slots = len(packs)
    pack_rows = held * (nonzero + 1) * LANES
    width = slots * held * LANES
    columns = width + LANES
    part = jax.ShapeDtypeStruct((width, columns), jnp.bfloat16)
    out_shape = [part, part]
    if last:
        out_shape.append(jax.ShapeDtypeStruct((width, columns), jnp.float32))

    def body(*refs):
        compose_kernel(first, last, base, steps, held, nonzero, slots, *refs)

    done = pl.pallas_call(
        body,
        in_specs=[SMEM] * 3 + [VMEM if last else HBM] * slots + [VMEM] * (1 + len(state)),
        out_specs=[VMEM] * len(out_shape),
        out_shape=out_shape,
        scratch_shapes=[
            pltpu.VMEM((width, columns), jnp.float32),
            pltpu.VMEM((LANES, columns), jnp.float32),
        ]
        + [
            pltpu.VMEM((slots, steps, pack_rows, LANES), jnp.float32),
            pltpu.SemaphoreType.DMA((slots, steps)),
        ]
        * (not last),
        cost_estimate=pl.CostEstimate(
            flops=steps * 2 * width * columns * 3 * (nonzero + 1) * LANES,
            transcendentals=0,
            bytes_accessed=4 * slots * steps * pack_rows * LANES,
        ),
        input_output_aliases={} if first else {slots + 4: 0, slots + 5: 1},
        compiler_params=pltpu.CompilerParams(vmem_limit_bytes=36 << 20),
        name="compose",
    )(places, pattern, sites, *[p if last else in_hbm(p) for p in packs], targets, *state)
    return done[2] if last else done


def hop_kernel(whole, start, end):
    blocks = start.shape[0]
    for r in range(blocks):
        rows = pl.ds(r * LANES, LANES)
        total = whole[rows, pl.ds(blocks * LANES, LANES)]
        for c in range(blocks):
            total = total + whole[rows, pl.ds(c * LANES, LANES)] * start[pl.ds(c, 1), :]
        end[pl.ds(r, 1), :] = lane_sums(total)


def hop(whole, start):
    return pl.pallas_call(
        hop_kernel,
        in_specs=[VMEM, VMEM],
        out_specs=VMEM,
        out_shape=jax.ShapeDtypeStruct(start.shape, jnp.float32),
        compiler_params=pltpu.CompilerParams(vmem_limit_bytes=2 << 20),
        name="hop",
    )(whole, start)


def fetches(packs, sizes, slots, store, sems):
    rows, steps = store.shape[2], []
    for c, size in enumerate(sizes):
        for i in range(size):
            t = len(steps)
            steps.append(
                [
                    pltpu.make_async_copy(
                        packs[c * slots + s].at[pl.ds(i * rows, rows), :],
                        store.at[s, t],
                        sems.at[s, t],
                    )
                    for s in range(slots)
                ]
            )
    return [copy for step in steps for copy in step]


def stage(sizes, pack_rows, packs, after):
    slots, steps = len(packs[0]), sum(sizes)

    def body(*refs):
        copies = fetches(refs, sizes, slots, refs[-2], refs[-1])
        for copy in copies:
            copy.start()
        for copy in copies:
            copy.wait()

    shape = (slots, steps, pack_rows, LANES)
    return pl.pallas_call(
        body,
        in_specs=[HBM] * (slots * len(sizes)) + [VMEM],
        out_specs=VMEM,
        out_shape=jax.ShapeDtypeStruct(shape, jnp.float32),
        scratch_shapes=[pltpu.SemaphoreType.DMA((slots, steps))],
        cost_estimate=pl.CostEstimate(
            flops=0, transcendentals=0, bytes_accessed=8 * math.prod(shape)
        ),
        compiler_params=pltpu.CompilerParams(vmem_limit_bytes=24 << 20),
        name="stage",
    )(*[in_hbm(p) for pack in packs for p in pack], after)


def segment_kernel(held, nonzero, sizes, slots, places, pattern, owner, store, *refs):
    packs, refs = refs[: slots * len(sizes)], refs[slots * len(sizes) :]
    targets, sites, weights, start, parcels, mean, predicted, rest, sems = refs
    near, far = store.shape[1], rest.shape[1]
    for copy in fetches(packs, sizes, slots, rest, sems):
        copy.start()
    mean[...] = start[...]
    mine = owner[0] == 1

    def step(t, misfit, load):
        innovation = filter_step(
            t, held, nonzero, places, pattern, load, targets, sites, mean, predicted
        )
        for s in range(slots):
            for h in range(held):
                row = mean[pl.ds(held * places[s] + h, 1), :]
                parcels[s, pl.ds(t * held + h, 1), :] = jnp.where(mine, row, 0.0)
        return misfit + innovation * innovation * weights[pl.ds(t, 1), :]

    def near_step(t, misfit):
        return step(t, misfit, lambda s, at: store[s, t, at, :])

    def far_step(t, misfit):
        for s in range(slots):
            rows = pl.ds(0, rest.shape[2])
            pltpu.make_async_copy(packs[s].at[rows, :], rest.at[s, t], sems.at[s, t]).wait()
        return step(near + t, misfit, lambda s, at: rest[s, t, at, :])

    misfit = lax.fori_loop(0, near, near_step, jnp.zeros((1, LANES), jnp.float32))
    misfit = lax.fori_loop(0, far, far_step, misfit)
    for s in range(slots):
        parcels[s, pl.ds((near + far) * held, 1), :] = jnp.where(mine, misfit, 0.0)


def run_segment(
    held, nonzero, sizes, places, pattern, owner, store, packs, targets, sites, weights, start
):
    slots, near, rows = store.shape[:3]
    far = sum(sizes)

    def body(*refs):
        segment_kernel(held, nonzero, sizes, slots, *refs)

    return pl.pallas_call(
        body,
        in_specs=[SMEM] * 3 + [VMEM] + [HBM] * (slots * len(sizes)) + [VMEM] * 4,
        out_specs=VMEM,
        out_shape=jax.ShapeDtypeStruct((slots, (near + far) * held + 1, LANES), jnp.float32),
        scratch_shapes=[
            pltpu.VMEM(start.shape, jnp.float32),
            pltpu.VMEM(start.shape, jnp.float32),
            pltpu.VMEM((slots, far, rows, LANES), jnp.float32),
            pltpu.SemaphoreType.DMA((slots, far)),
        ],
        compiler_params=pltpu.CompilerParams(vmem_limit_bytes=32 << 20),
        name="segment",
    )(
        places,
        pattern,
        owner,
        store,
        *[in_hbm(p) for pack in packs for p in pack],
        targets,
        sites,
        weights,
        start,
    )


def filter_step(t, held, nonzero, places, pattern, load, targets, sites, mean, predicted):
    blocks = mean.shape[0]
    slots = blocks // held
    for s in range(slots):
        for h in range(held):
            row = held * places[s] + h
            total = None
            for j in range(nonzero):
                column = pattern[t, row * nonzero + j]
                block = load(s, pl.ds((h * nonzero + j) * LANES, LANES))
                part = block * mean[pl.ds(column, 1), :]
                total = part if total is None else total + part
            predicted[pl.ds(row, 1), :] = lane_sums(total)
    flat = ORDER * sites[pl.ds(t, 1), :]
    lane = jnp.broadcast_to(flat % LANES, (blocks, LANES))
    picked = jnp.take_along_axis(predicted[...], lane, axis=1)
    block = lax.broadcasted_iota(jnp.int32, (blocks, LANES), 0)
    picked = jnp.where(block == flat // LANES, picked, 0.0)
    innovation = targets[pl.ds(t, 1), :] - jnp.sum(picked, axis=0, keepdims=True)
    for s in range(slots):
        for h in range(held):
            row = held * places[s] + h
            gain = load(s, pl.ds((held * nonzero + h) * LANES, LANES))
            updated = predicted[pl.ds(row, 1), :] + lane_sums(gain * innovation)
            mean[pl.ds(row, 1), :] = updated
    return innovation


def on_device(
    observations,
    sites,
    pattern,
    block_values,
    gains,
    variances,
    monotone_bend_strength,
    initial_mean,
):
    segments, rows = lax.axis_size("tm"), lax.axis_size("row")
    tm, row = lax.axis_index("tm"), lax.axis_index("row")
    steps, held, nonzero = block_values.shape[:3]
    even = tm % 2 == 0

    low = (rows - 1) // 2
    order_even = sorted(range(rows), key=lambda z: (abs(z - low), z))
    order_odd = [rows - 1 - z for z in order_even]

    def order(t):
        return order_even if t % 2 == 0 else order_odd

    def flat(t, z):
        return t * rows + z

    both = ("tm", "row")

    def meet(shard):
        moved = [shard]
        for k in range(1, rows):
            pairs = [(flat(t, order(t)[k]), flat(t, order(t)[0])) for t in range(segments)]
            moved.append(lax.ppermute(shard, both, pairs))
        return moved

    places = jnp.where(
        even, jnp.array(order_even, jnp.int32), jnp.array(order_odd, jnp.int32)
    )
    scale = monotone_bend_strength[0]
    bent = jnp.tanh(observations)
    targets = observations + scale * bent
    log_jacobian = jnp.log(1.0 + scale * (1.0 - bent * bent))
    flat_pattern = pattern.reshape(steps, -1)

    sizes = CHUNKS if sum(CHUNKS) == steps else (1,) * steps
    pack_rows = held * (nonzero + 1) * LANES
    packs, base = [], 0
    for i, size in enumerate(sizes):
        blocks = block_values[base : base + size].reshape(size, -1, LANES)
        pack = jnp.concatenate([blocks, gains[base : base + size]], axis=1)
        pack = pack.reshape(size * pack_rows, LANES)
        if i == 0:
            first = initial_mean.reshape(held, LANES)
            pack = jnp.concatenate([pack, jnp.pad(first, ((0, -held % 8), (0, 0)))])
        packs.append(pack)
        base += size

    packs[:2] = [meet(pack) for pack in packs[:2]]
    state, base = (), 0
    for i, size in enumerate(sizes):
        state = compose(
            i == 0,
            i == len(sizes) - 1,
            base,
            size,
            held,
            nonzero,
            places,
            flat_pattern,
            sites,
            packs[i],
            targets,
            state,
        )
        base += size
        for k in (i + 2, i + 3):
            if k == i + 2 < len(sizes) - 1 or k == i + 3 == len(sizes) - 1:
                packs[k], *state = lax.optimization_barrier((packs[k], *state))
                packs[k] = meet(packs[k])

    starts = [p[sizes[0] * pack_rows :][:held] for p in packs[0]]
    by_even = [starts[order_even.index(z)] for z in range(rows)]
    by_odd = [starts[order_odd.index(z)] for z in range(rows)]
    start = jnp.where(even, jnp.concatenate(by_even), jnp.concatenate(by_odd))

    mean, begin = start, jnp.where(tm == 0, start, 0.0)
    for t in range(segments - 1):
        pair = [(flat(t, order(t)[0]), flat(t + 1, order(t + 1)[0]))]
        ended = hop(state, mean)
        mean = lax.ppermute(ended, both, pair)
        begin = begin + mean
    store = stage(sizes[:STAGED], pack_rows, packs[:STAGED], ended)
    owner = (row == places[:1]).astype(jnp.int32)
    local = run_segment(
        held,
        nonzero,
        sizes[STAGED:],
        places,
        flat_pattern,
        owner,
        store,
        packs[STAGED:],
        targets,
        sites,
        1.0 / variances,
        begin,
    )

    while local.shape[0] > 1:
        half = local.shape[0] // 2
        pairs = [
            (flat(t, order(t)[i]), flat(t, order(t)[i + half]))
            for t in range(segments)
            for i in range(0, rows, 2 * half)
        ]
        local = local[:half] + lax.ppermute(local[half:], both, pairs)
    own_filtered = local[0, : steps * held].reshape(steps, held * LANES)

    term = jnp.sum(log_jacobian - 0.5 * jnp.log(variances), axis=0, keepdims=True)
    term = term - 0.5 * local[0, steps * held :]
    if segments & (segments - 1):
        term = lax.psum(term, "tm")
    else:
        reach = 1
        while reach < segments:
            term = term + lax.ppermute(term, "tm", [(t, t ^ reach) for t in range(segments)])
            reach *= 2
    count = observations.size * segments
    evidence = jnp.sum(term) / count - 0.5 * math.log(2.0 * math.pi)
    return own_filtered, evidence.reshape(1)


def solution(mesh):
    in_specs = (
        P("tm", None),
        P("tm", None),
        P("tm", None, None),
        P("tm", "row", None, None, None),
        P("tm", "row", None),
        P("tm", None),
        P(),
        P("row"),
    )
    out_specs = (P("tm", "row"), P())
    return jax.shard_map(
        on_device, mesh=mesh, in_specs=in_specs, out_specs=out_specs, check_vma=False
    )
```

```python
import math

import jax
import jax.numpy as jnp
from jax import lax
from jax.experimental import pallas as pl
from jax.experimental.pallas import tpu as pltpu
from jax.sharding import PartitionSpec as P

ORDER = 4
LANES = 128
CHUNKS = (1, 2, 2, 2, 1)
STAGED = 2
VMEM = pl.BlockSpec(memory_space=pltpu.VMEM)
HBM = pl.BlockSpec(memory_space=pltpu.HBM)
SMEM = pl.BlockSpec(memory_space=pltpu.SMEM)


def in_hbm(x):
    return pltpu.with_memory_space_constraint(x, pltpu.HBM)


def split(x):
    high = x.astype(jnp.bfloat16)
    return high, (x - high.astype(jnp.float32)).astype(jnp.bfloat16)


def matmul(a, b):
    return jnp.dot(a, b, preferred_element_type=jnp.float32)


def lane_sums(block):
    return jnp.sum(block.T, axis=0, keepdims=True)


def aligned(row):
    return pl.ds(pl.multiple_of(row * LANES, LANES), LANES)


def compose_kernel(first, last, base, steps, held, nonzero, slots, places, pattern, sites, *refs):
    packs, refs = refs[:slots], refs[slots:]
    targets, refs = refs[0], refs[1:]
    if not first:
        refs = refs[2:]
    high, low, refs = refs[0], refs[1], refs[2:]
    if last:
        whole, refs = refs[0], refs[1:]
    through, seen = refs
    width, columns = high.shape
    pack_rows = held * (nonzero + 1) * LANES
    gain_row = held * nonzero * LANES

    def load(s, t, at):
        start = pl.multiple_of(t * pack_rows + at.start, LANES)
        return packs[s][pl.ds(start, at.size), :]

    def step(t, carry):
        def block_row(s, h):
            row = held * places[s] + h
            picks = [aligned(pattern[base + t, row * nonzero + j]) for j in range(nonzero)]
            if first:
                for j in range(nonzero):
                    block = load(s, t, aligned(h * nonzero + j))
                    through[aligned(row), picks[j]] = through[aligned(row), picks[j]] + block
                return
            parts = [split(load(s, t, aligned(h * nonzero + j))) for j in range(nonzero)]
            up = [p[0] for p in parts]
            down = [p[1] for p in parts]
            tops = [high[pick, :] for pick in picks]
            bottoms = [low[pick, :] for pick in picks]
            through[aligned(row), :] = matmul(
                jnp.concatenate(up + down + up, axis=1),
                jnp.concatenate(tops + tops + bottoms),
            )

        if first:
            through[...] = jnp.zeros_like(through)
        for s in range(slots):
            for h in range(held):
                block_row(s, h)

        def pick_rows(i, carry):
            for u in range(32):
                k = i * 32 + u
                seen[pl.ds(k, 1), :] = through[pl.ds(ORDER * sites[base + t, k], 1), :]
            return carry

        lax.fori_loop(0, LANES // 32, pick_rows, 0)
        target = jnp.broadcast_to(targets[pl.ds(base + t, 1), :], (LANES, LANES)).T
        lane = lax.broadcasted_iota(jnp.int32, (LANES, LANES), 1)
        offset = pl.ds(width, LANES)
        seen[:, offset] = seen[:, offset] - jnp.where(lane == 0, target, 0.0)
        top, bottom = split(seen[...])
        halves = [split(load(s, t, pl.ds(gain_row, held * LANES))) for s in range(slots)]
        left = jnp.concatenate([jnp.concatenate([a, b, a], axis=1) for a, b in halves])
        moved = matmul(left, jnp.concatenate([top, top, bottom]))
        for s in range(slots):
            for h in range(held):
                here = aligned(held * places[s] + h)
                at = (s * held + h) * LANES
                new = through[here, :] - moved[at : at + LANES]
                if last:

                    @pl.when(t == steps - 1)
                    def _(here=here, new=new):
                        whole[here, :] = new

                if not last or steps > 1:
                    a, b = split(new)
                    high[here, :] = a
                    low[here, :] = b
        return carry

    lax.fori_loop(0, steps, step, 0)


def compose(first, last, base, steps, held, nonzero, places, pattern, sites, packs, targets, state):
    slots = len(packs)
    pack_rows = held * (nonzero + 1) * LANES
    width = slots * held * LANES
    columns = width + LANES
    part = jax.ShapeDtypeStruct((width, columns), jnp.bfloat16)
    out_shape = [part, part]
    if last:
        out_shape.append(jax.ShapeDtypeStruct((width, columns), jnp.float32))

    def body(*refs):
        compose_kernel(first, last, base, steps, held, nonzero, slots, *refs)

    done = pl.pallas_call(
        body,
        in_specs=[SMEM] * 3 + [VMEM] * (slots + 1 + len(state)),
        out_specs=[VMEM] * len(out_shape),
        out_shape=out_shape,
        scratch_shapes=[
            pltpu.VMEM((width, columns), jnp.float32),
            pltpu.VMEM((LANES, columns), jnp.float32),
        ],
        cost_estimate=pl.CostEstimate(
            flops=steps * 2 * width * columns * 3 * (nonzero + 1) * LANES,
            transcendentals=0,
            bytes_accessed=4 * slots * steps * pack_rows * LANES,
        ),
        input_output_aliases={} if first else {slots + 4: 0, slots + 5: 1},
        compiler_params=pltpu.CompilerParams(vmem_limit_bytes=36 << 20),
        name="compose",
    )(places, pattern, sites, *packs, targets, *state)
    return done[2] if last else done


def hop_kernel(whole, start, end):
    blocks = start.shape[0]
    for r in range(blocks):
        rows = pl.ds(r * LANES, LANES)
        total = whole[rows, pl.ds(blocks * LANES, LANES)]
        for c in range(blocks):
            total = total + whole[rows, pl.ds(c * LANES, LANES)] * start[pl.ds(c, 1), :]
        end[pl.ds(r, 1), :] = lane_sums(total)


def hop(whole, start):
    return pl.pallas_call(
        hop_kernel,
        in_specs=[VMEM, VMEM],
        out_specs=VMEM,
        out_shape=jax.ShapeDtypeStruct(start.shape, jnp.float32),
        compiler_params=pltpu.CompilerParams(vmem_limit_bytes=2 << 20),
        name="hop",
    )(whole, start)


def fetches(packs, sizes, slots, store, sems):
    rows, steps = store.shape[2], []
    for c, size in enumerate(sizes):
        for i in range(size):
            t = len(steps)
            steps.append(
                [
                    pltpu.make_async_copy(
                        packs[c * slots + s].at[pl.ds(i * rows, rows), :],
                        store.at[s, t],
                        sems.at[s, t],
                    )
                    for s in range(slots)
                ]
            )
    return [copy for step in steps for copy in step]


def stage(sizes, pack_rows, packs, after):
    slots, steps = len(packs[0]), sum(sizes)

    def body(*refs):
        copies = fetches(refs, sizes, slots, refs[-2], refs[-1])
        for copy in copies:
            copy.start()
        for copy in copies:
            copy.wait()

    shape = (slots, steps, pack_rows, LANES)
    return pl.pallas_call(
        body,
        in_specs=[HBM] * (slots * len(sizes)) + [VMEM],
        out_specs=VMEM,
        out_shape=jax.ShapeDtypeStruct(shape, jnp.float32),
        scratch_shapes=[pltpu.SemaphoreType.DMA((slots, steps))],
        cost_estimate=pl.CostEstimate(
            flops=0, transcendentals=0, bytes_accessed=8 * math.prod(shape)
        ),
        compiler_params=pltpu.CompilerParams(vmem_limit_bytes=24 << 20),
        name="stage",
    )(*[in_hbm(p) for pack in packs for p in pack], after)


def segment_kernel(held, nonzero, sizes, slots, places, pattern, owner, store, *refs):
    packs, refs = refs[: slots * len(sizes)], refs[slots * len(sizes) :]
    targets, sites, weights, start, parcels, mean, predicted, rest, sems = refs
    near, far = store.shape[1], rest.shape[1]
    for copy in fetches(packs, sizes, slots, rest, sems):
        copy.start()
    mean[...] = start[...]
    mine = owner[0] == 1

    def step(t, misfit, load):
        innovation = filter_step(
            t, held, nonzero, places, pattern, load, targets, sites, mean, predicted
        )
        for s in range(slots):
            for h in range(held):
                row = mean[pl.ds(held * places[s] + h, 1), :]
                parcels[s, pl.ds(t * held + h, 1), :] = jnp.where(mine, row, 0.0)
        return misfit + innovation * innovation * weights[pl.ds(t, 1), :]

    def near_step(t, misfit):
        return step(t, misfit, lambda s, at: store[s, t, at, :])

    def far_step(t, misfit):
        for s in range(slots):
            rows = pl.ds(0, rest.shape[2])
            pltpu.make_async_copy(packs[s].at[rows, :], rest.at[s, t], sems.at[s, t]).wait()
        return step(near + t, misfit, lambda s, at: rest[s, t, at, :])

    misfit = lax.fori_loop(0, near, near_step, jnp.zeros((1, LANES), jnp.float32))
    misfit = lax.fori_loop(0, far, far_step, misfit)
    for s in range(slots):
        parcels[s, pl.ds((near + far) * held, 1), :] = jnp.where(mine, misfit, 0.0)


def run_segment(
    held, nonzero, sizes, places, pattern, owner, store, packs, targets, sites, weights, start
):
    slots, near, rows = store.shape[:3]
    far = sum(sizes)

    def body(*refs):
        segment_kernel(held, nonzero, sizes, slots, *refs)

    return pl.pallas_call(
        body,
        in_specs=[SMEM] * 3 + [VMEM] + [HBM] * (slots * len(sizes)) + [VMEM] * 4,
        out_specs=VMEM,
        out_shape=jax.ShapeDtypeStruct((slots, (near + far) * held + 1, LANES), jnp.float32),
        scratch_shapes=[
            pltpu.VMEM(start.shape, jnp.float32),
            pltpu.VMEM(start.shape, jnp.float32),
            pltpu.VMEM((slots, far, rows, LANES), jnp.float32),
            pltpu.SemaphoreType.DMA((slots, far)),
        ],
        compiler_params=pltpu.CompilerParams(vmem_limit_bytes=32 << 20),
        name="segment",
    )(
        places,
        pattern,
        owner,
        store,
        *[in_hbm(p) for pack in packs for p in pack],
        targets,
        sites,
        weights,
        start,
    )


def filter_step(t, held, nonzero, places, pattern, load, targets, sites, mean, predicted):
    blocks = mean.shape[0]
    slots = blocks // held
    for s in range(slots):
        for h in range(held):
            row = held * places[s] + h
            total = None
            for j in range(nonzero):
                column = pattern[t, row * nonzero + j]
                block = load(s, pl.ds((h * nonzero + j) * LANES, LANES))
                part = block * mean[pl.ds(column, 1), :]
                total = part if total is None else total + part
            predicted[pl.ds(row, 1), :] = lane_sums(total)
    flat = ORDER * sites[pl.ds(t, 1), :]
    lane = jnp.broadcast_to(flat % LANES, (blocks, LANES))
    picked = jnp.take_along_axis(predicted[...], lane, axis=1)
    block = lax.broadcasted_iota(jnp.int32, (blocks, LANES), 0)
    picked = jnp.where(block == flat // LANES, picked, 0.0)
    innovation = targets[pl.ds(t, 1), :] - jnp.sum(picked, axis=0, keepdims=True)
    for s in range(slots):
        for h in range(held):
            row = held * places[s] + h
            gain = load(s, pl.ds((held * nonzero + h) * LANES, LANES))
            updated = predicted[pl.ds(row, 1), :] + lane_sums(gain * innovation)
            mean[pl.ds(row, 1), :] = updated
    return innovation


def on_device(
    observations,
    sites,
    pattern,
    block_values,
    gains,
    variances,
    monotone_bend_strength,
    initial_mean,
):
    segments, rows = lax.axis_size("tm"), lax.axis_size("row")
    tm, row = lax.axis_index("tm"), lax.axis_index("row")
    steps, held, nonzero = block_values.shape[:3]
    even = tm % 2 == 0

    low = (rows - 1) // 2
    order_even = sorted(range(rows), key=lambda z: (abs(z - low), z))
    order_odd = [rows - 1 - z for z in order_even]

    def order(t):
        return order_even if t % 2 == 0 else order_odd

    def flat(t, z):
        return t * rows + z

    both = ("tm", "row")

    def meet(shard):
        moved = [shard]
        for k in range(1, rows):
            pairs = [(flat(t, order(t)[k]), flat(t, order(t)[0])) for t in range(segments)]
            moved.append(lax.ppermute(shard, both, pairs))
        return moved

    places = jnp.where(
        even, jnp.array(order_even, jnp.int32), jnp.array(order_odd, jnp.int32)
    )
    scale = monotone_bend_strength[0]
    bent = jnp.tanh(observations)
    targets = observations + scale * bent
    log_jacobian = jnp.log(1.0 + scale * (1.0 - bent * bent))
    flat_pattern = pattern.reshape(steps, -1)

    sizes = CHUNKS if sum(CHUNKS) == steps else (1,) * steps
    pack_rows = held * (nonzero + 1) * LANES
    packs, base = [], 0
    for i, size in enumerate(sizes):
        blocks = block_values[base : base + size].reshape(size, -1, LANES)
        pack = jnp.concatenate([blocks, gains[base : base + size]], axis=1)
        pack = pack.reshape(size * pack_rows, LANES)
        if i == 0:
            first = initial_mean.reshape(held, LANES)
            pack = jnp.concatenate([pack, jnp.pad(first, ((0, -held % 8), (0, 0)))])
        packs.append(pack)
        base += size

    packs[:2] = [meet(pack) for pack in packs[:2]]
    state, base = (), 0
    for i, size in enumerate(sizes):
        state = compose(
            i == 0,
            i == len(sizes) - 1,
            base,
            size,
            held,
            nonzero,
            places,
            flat_pattern,
            sites,
            packs[i],
            targets,
            state,
        )
        base += size
        for k in (i + 2, i + 3):
            if k == i + 2 < len(sizes) - 1 or k == i + 3 == len(sizes) - 1:
                packs[k], *state = lax.optimization_barrier((packs[k], *state))
                packs[k] = meet(packs[k])

    starts = [p[sizes[0] * pack_rows :][:held] for p in packs[0]]
    by_even = [starts[order_even.index(z)] for z in range(rows)]
    by_odd = [starts[order_odd.index(z)] for z in range(rows)]
    start = jnp.where(even, jnp.concatenate(by_even), jnp.concatenate(by_odd))

    mean, begin = start, jnp.where(tm == 0, start, 0.0)
    for t in range(segments - 1):
        pair = [(flat(t, order(t)[0]), flat(t + 1, order(t + 1)[0]))]
        ended = hop(state, mean)
        mean = lax.ppermute(ended, both, pair)
        begin = begin + mean
    store = stage(sizes[:STAGED], pack_rows, packs[:STAGED], ended)
    owner = (row == places[:1]).astype(jnp.int32)
    local = run_segment(
        held,
        nonzero,
        sizes[STAGED:],
        places,
        flat_pattern,
        owner,
        store,
        packs[STAGED:],
        targets,
        sites,
        1.0 / variances,
        begin,
    )

    while local.shape[0] > 1:
        half = local.shape[0] // 2
        pairs = [
            (flat(t, order(t)[i]), flat(t, order(t)[i + half]))
            for t in range(segments)
            for i in range(0, rows, 2 * half)
        ]
        local = local[:half] + lax.ppermute(local[half:], both, pairs)
    own_filtered = local[0, : steps * held].reshape(steps, held * LANES)

    term = jnp.sum(log_jacobian - 0.5 * jnp.log(variances), axis=0, keepdims=True)
    term = term - 0.5 * local[0, steps * held :]
    if segments & (segments - 1):
        term = lax.psum(term, "tm")
    else:
        reach = 1
        while reach < segments:
            term = term + lax.ppermute(term, "tm", [(t, t ^ reach) for t in range(segments)])
            reach *= 2
    count = observations.size * segments
    evidence = jnp.sum(term) / count - 0.5 * math.log(2.0 * math.pi)
    return own_filtered, evidence.reshape(1)


def solution(mesh):
    in_specs = (
        P("tm", None),
        P("tm", None),
        P("tm", None, None),
        P("tm", "row", None, None, None),
        P("tm", "row", None),
        P("tm", None),
        P(),
        P("row"),
    )
    out_specs = (P("tm", "row"), P())
    return jax.shard_map(
        on_device, mesh=mesh, in_specs=in_specs, out_specs=out_specs, check_vma=False
    )
```

```python
import math

import jax
import jax.numpy as jnp
from jax import lax
from jax.experimental import pallas as pl
from jax.experimental.pallas import tpu as pltpu
from jax.sharding import PartitionSpec as P

ORDER = 4
LANES = 128
CHUNKS = (1, 2, 2, 2, 1)
STAGED = 2
VMEM = pl.BlockSpec(memory_space=pltpu.VMEM)
HBM = pl.BlockSpec(memory_space=pltpu.HBM)
SMEM = pl.BlockSpec(memory_space=pltpu.SMEM)


def in_hbm(x):
    return pltpu.with_memory_space_constraint(x, pltpu.HBM)


def split(x):
    high = x.astype(jnp.bfloat16)
    return high, (x - high.astype(jnp.float32)).astype(jnp.bfloat16)


def matmul(a, b):
    return jnp.dot(a, b, preferred_element_type=jnp.float32)


def lane_sums(block):
    return jnp.sum(block.T, axis=0, keepdims=True)


def aligned(row):
    return pl.ds(pl.multiple_of(row * LANES, LANES), LANES)


def compose_kernel(first, last, base, steps, held, nonzero, slots, places, pattern, sites, *refs):
    packs, refs = refs[:slots], refs[slots:]
    targets, refs = refs[0], refs[1:]
    if not first:
        refs = refs[2:]
    high, low, refs = refs[0], refs[1], refs[2:]
    if last:
        whole, refs = refs[0], refs[1:]
    through, seen = refs
    width, columns = high.shape
    pack_rows = held * (nonzero + 1) * LANES
    gain_row = held * nonzero * LANES

    def load(s, t, at):
        start = pl.multiple_of(t * pack_rows + at.start, LANES)
        return packs[s][pl.ds(start, at.size), :]

    def step(t, carry):
        def block_row(s, h):
            row = held * places[s] + h
            picks = [aligned(pattern[base + t, row * nonzero + j]) for j in range(nonzero)]
            if first:
                for j in range(nonzero):
                    block = load(s, t, aligned(h * nonzero + j))
                    through[aligned(row), picks[j]] = through[aligned(row), picks[j]] + block
                return
            parts = [split(load(s, t, aligned(h * nonzero + j))) for j in range(nonzero)]
            up = [p[0] for p in parts]
            down = [p[1] for p in parts]
            tops = [high[pick, :] for pick in picks]
            bottoms = [low[pick, :] for pick in picks]
            through[aligned(row), :] = matmul(
                jnp.concatenate(up + down + up, axis=1),
                jnp.concatenate(tops + tops + bottoms),
            )

        if first:
            through[...] = jnp.zeros_like(through)
        for s in range(slots):
            for h in range(held):
                block_row(s, h)

        def pick_rows(i, carry):
            for u in range(32):
                k = i * 32 + u
                seen[pl.ds(k, 1), :] = through[pl.ds(ORDER * sites[base + t, k], 1), :]
            return carry

        lax.fori_loop(0, LANES // 32, pick_rows, 0)
        target = jnp.broadcast_to(targets[pl.ds(base + t, 1), :], (LANES, LANES)).T
        lane = lax.broadcasted_iota(jnp.int32, (LANES, LANES), 1)
        offset = pl.ds(width, LANES)
        seen[:, offset] = seen[:, offset] - jnp.where(lane == 0, target, 0.0)
        top, bottom = split(seen[...])
        halves = [split(load(s, t, pl.ds(gain_row, held * LANES))) for s in range(slots)]
        left = jnp.concatenate([jnp.concatenate([a, b, a], axis=1) for a, b in halves])
        moved = matmul(left, jnp.concatenate([top, top, bottom]))
        for s in range(slots):
            for h in range(held):
                here = aligned(held * places[s] + h)
                at = (s * held + h) * LANES
                new = through[here, :] - moved[at : at + LANES]
                if last:

                    @pl.when(t == steps - 1)
                    def _(here=here, new=new):
                        whole[here, :] = new

                if not last or steps > 1:
                    a, b = split(new)
                    high[here, :] = a
                    low[here, :] = b
        return carry

    lax.fori_loop(0, steps, step, 0)


def compose(first, last, base, steps, held, nonzero, places, pattern, sites, packs, targets, state):
    slots = len(packs)
    pack_rows = held * (nonzero + 1) * LANES
    width = slots * held * LANES
    columns = width + LANES
    part = jax.ShapeDtypeStruct((width, columns), jnp.bfloat16)
    out_shape = [part, part]
    if last:
        out_shape.append(jax.ShapeDtypeStruct((width, columns), jnp.float32))

    def body(*refs):
        compose_kernel(first, last, base, steps, held, nonzero, slots, *refs)

    done = pl.pallas_call(
        body,
        in_specs=[SMEM] * 3 + [VMEM] * (slots + 1 + len(state)),
        out_specs=[VMEM] * len(out_shape),
        out_shape=out_shape,
        scratch_shapes=[
            pltpu.VMEM((width, columns), jnp.float32),
            pltpu.VMEM((LANES, columns), jnp.float32),
        ],
        cost_estimate=pl.CostEstimate(
            flops=steps * 2 * width * columns * 3 * (nonzero + 1) * LANES,
            transcendentals=0,
            bytes_accessed=4 * slots * steps * pack_rows * LANES,
        ),
        input_output_aliases={} if first else {slots + 4: 0, slots + 5: 1},
        compiler_params=pltpu.CompilerParams(vmem_limit_bytes=36 << 20),
        name="compose",
    )(places, pattern, sites, *packs, targets, *state)
    return done[2] if last else done


def hop_kernel(whole, start, end):
    blocks = start.shape[0]
    for r in range(blocks):
        rows = pl.ds(r * LANES, LANES)
        total = whole[rows, pl.ds(blocks * LANES, LANES)]
        for c in range(blocks):
            total = total + whole[rows, pl.ds(c * LANES, LANES)] * start[pl.ds(c, 1), :]
        end[pl.ds(r, 1), :] = lane_sums(total)


def hop(whole, start):
    return pl.pallas_call(
        hop_kernel,
        in_specs=[VMEM, VMEM],
        out_specs=VMEM,
        out_shape=jax.ShapeDtypeStruct(start.shape, jnp.float32),
        compiler_params=pltpu.CompilerParams(vmem_limit_bytes=2 << 20),
        name="hop",
    )(whole, start)


def fetches(packs, sizes, slots, store, sems):
    rows, steps = store.shape[2], []
    for c, size in enumerate(sizes):
        for i in range(size):
            t = len(steps)
            steps.append(
                [
                    pltpu.make_async_copy(
                        packs[c * slots + s].at[pl.ds(i * rows, rows), :],
                        store.at[s, t],
                        sems.at[s, t],
                    )
                    for s in range(slots)
                ]
            )
    return [copy for step in steps for copy in step]


def stage(sizes, pack_rows, packs, after):
    slots, steps = len(packs[0]), sum(sizes)

    def body(*refs):
        copies = fetches(refs, sizes, slots, refs[-2], refs[-1])
        for copy in copies:
            copy.start()
        for copy in copies:
            copy.wait()

    shape = (slots, steps, pack_rows, LANES)
    return pl.pallas_call(
        body,
        in_specs=[HBM] * (slots * len(sizes)) + [VMEM],
        out_specs=VMEM,
        out_shape=jax.ShapeDtypeStruct(shape, jnp.float32),
        scratch_shapes=[pltpu.SemaphoreType.DMA((slots, steps))],
        cost_estimate=pl.CostEstimate(
            flops=0, transcendentals=0, bytes_accessed=8 * math.prod(shape)
        ),
        compiler_params=pltpu.CompilerParams(vmem_limit_bytes=24 << 20),
        name="stage",
    )(*[in_hbm(p) for pack in packs for p in pack], after)


def segment_kernel(held, nonzero, sizes, slots, places, pattern, owner, store, *refs):
    packs, refs = refs[: slots * len(sizes)], refs[slots * len(sizes) :]
    targets, sites, weights, start, parcels, mean, predicted, rest, sems = refs
    near, far = store.shape[1], rest.shape[1]
    for copy in fetches(packs, sizes, slots, rest, sems):
        copy.start()
    mean[...] = start[...]
    mine = owner[0] == 1

    def step(t, misfit, load):
        innovation = filter_step(
            t, held, nonzero, places, pattern, load, targets, sites, mean, predicted
        )
        for s in range(slots):
            for h in range(held):
                row = mean[pl.ds(held * places[s] + h, 1), :]
                parcels[s, pl.ds(t * held + h, 1), :] = jnp.where(mine, row, 0.0)
        return misfit + innovation * innovation * weights[pl.ds(t, 1), :]

    def near_step(t, misfit):
        return step(t, misfit, lambda s, at: store[s, t, at, :])

    def far_step(t, misfit):
        for s in range(slots):
            rows = pl.ds(0, rest.shape[2])
            pltpu.make_async_copy(packs[s].at[rows, :], rest.at[s, t], sems.at[s, t]).wait()
        return step(near + t, misfit, lambda s, at: rest[s, t, at, :])

    misfit = lax.fori_loop(0, near, near_step, jnp.zeros((1, LANES), jnp.float32))
    misfit = lax.fori_loop(0, far, far_step, misfit)
    for s in range(slots):
        parcels[s, pl.ds((near + far) * held, 1), :] = jnp.where(mine, misfit, 0.0)


def run_segment(
    held, nonzero, sizes, places, pattern, owner, store, packs, targets, sites, weights, start
):
    slots, near, rows = store.shape[:3]
    far = sum(sizes)

    def body(*refs):
        segment_kernel(held, nonzero, sizes, slots, *refs)

    return pl.pallas_call(
        body,
        in_specs=[SMEM] * 3 + [VMEM] + [HBM] * (slots * len(sizes)) + [VMEM] * 4,
        out_specs=VMEM,
        out_shape=jax.ShapeDtypeStruct((slots, (near + far) * held + 1, LANES), jnp.float32),
        scratch_shapes=[
            pltpu.VMEM(start.shape, jnp.float32),
            pltpu.VMEM(start.shape, jnp.float32),
            pltpu.VMEM((slots, far, rows, LANES), jnp.float32),
            pltpu.SemaphoreType.DMA((slots, far)),
        ],
        compiler_params=pltpu.CompilerParams(vmem_limit_bytes=32 << 20),
        name="segment",
    )(
        places,
        pattern,
        owner,
        store,
        *[in_hbm(p) for pack in packs for p in pack],
        targets,
        sites,
        weights,
        start,
    )


def filter_step(t, held, nonzero, places, pattern, load, targets, sites, mean, predicted):
    blocks = mean.shape[0]
    slots = blocks // held
    for s in range(slots):
        for h in range(held):
            row = held * places[s] + h
            total = None
            for j in range(nonzero):
                column = pattern[t, row * nonzero + j]
                block = load(s, pl.ds((h * nonzero + j) * LANES, LANES))
                part = block * mean[pl.ds(column, 1), :]
                total = part if total is None else total + part
            predicted[pl.ds(row, 1), :] = lane_sums(total)
    flat = ORDER * sites[pl.ds(t, 1), :]
    lane = jnp.broadcast_to(flat % LANES, (blocks, LANES))
    picked = jnp.take_along_axis(predicted[...], lane, axis=1)
    block = lax.broadcasted_iota(jnp.int32, (blocks, LANES), 0)
    picked = jnp.where(block == flat // LANES, picked, 0.0)
    innovation = targets[pl.ds(t, 1), :] - jnp.sum(picked, axis=0, keepdims=True)
    for s in range(slots):
        for h in range(held):
            row = held * places[s] + h
            gain = load(s, pl.ds((held * nonzero + h) * LANES, LANES))
            updated = predicted[pl.ds(row, 1), :] + lane_sums(gain * innovation)
            mean[pl.ds(row, 1), :] = updated
    return innovation


def on_device(
    observations,
    sites,
    pattern,
    block_values,
    gains,
    variances,
    monotone_bend_strength,
    initial_mean,
):
    segments, rows = lax.axis_size("tm"), lax.axis_size("row")
    tm, row = lax.axis_index("tm"), lax.axis_index("row")
    steps, held, nonzero = block_values.shape[:3]
    even = tm % 2 == 0

    low = (rows - 1) // 2
    order_even = sorted(range(rows), key=lambda z: (abs(z - low), z))
    order_odd = [rows - 1 - z for z in order_even]

    def order(t):
        return order_even if t % 2 == 0 else order_odd

    def flat(t, z):
        return t * rows + z

    both = ("tm", "row")

    def meet(shard):
        moved = [shard]
        for k in range(1, rows):
            pairs = [(flat(t, order(t)[k]), flat(t, order(t)[0])) for t in range(segments)]
            moved.append(lax.ppermute(shard, both, pairs))
        return moved

    places = jnp.where(
        even, jnp.array(order_even, jnp.int32), jnp.array(order_odd, jnp.int32)
    )
    scale = monotone_bend_strength[0]
    bent = jnp.tanh(observations)
    targets = observations + scale * bent
    log_jacobian = jnp.log(1.0 + scale * (1.0 - bent * bent))
    flat_pattern = pattern.reshape(steps, -1)

    sizes = CHUNKS if sum(CHUNKS) == steps else (1,) * steps
    pack_rows = held * (nonzero + 1) * LANES
    packs, base = [], 0
    for i, size in enumerate(sizes):
        blocks = block_values[base : base + size].reshape(size, -1, LANES)
        pack = jnp.concatenate([blocks, gains[base : base + size]], axis=1)
        pack = pack.reshape(size * pack_rows, LANES)
        if i == 0:
            first = initial_mean.reshape(held, LANES)
            pack = jnp.concatenate([pack, jnp.pad(first, ((0, -held % 8), (0, 0)))])
            pack, block_values, gains = lax.optimization_barrier((pack, block_values, gains))
        packs.append(pack)
        base += size

    packs[:2] = [meet(pack) for pack in packs[:2]]
    state, base = (), 0
    for i, size in enumerate(sizes):
        state = compose(
            i == 0,
            i == len(sizes) - 1,
            base,
            size,
            held,
            nonzero,
            places,
            flat_pattern,
            sites,
            packs[i],
            targets,
            state,
        )
        base += size
        for k in (i + 2, i + 3):
            if k == i + 2 < len(sizes) - 1 or k == i + 3 == len(sizes) - 1:
                packs[k], *state = lax.optimization_barrier((packs[k], *state))
                packs[k] = meet(packs[k])

    starts = [p[sizes[0] * pack_rows :][:held] for p in packs[0]]
    by_even = [starts[order_even.index(z)] for z in range(rows)]
    by_odd = [starts[order_odd.index(z)] for z in range(rows)]
    start = jnp.where(even, jnp.concatenate(by_even), jnp.concatenate(by_odd))

    mean, begin = start, jnp.where(tm == 0, start, 0.0)
    for t in range(segments - 1):
        pair = [(flat(t, order(t)[0]), flat(t + 1, order(t + 1)[0]))]
        ended = hop(state, mean)
        mean = lax.ppermute(ended, both, pair)
        begin = begin + mean
    store = stage(sizes[:STAGED], pack_rows, packs[:STAGED], ended)
    owner = (row == places[:1]).astype(jnp.int32)
    local = run_segment(
        held,
        nonzero,
        sizes[STAGED:],
        places,
        flat_pattern,
        owner,
        store,
        packs[STAGED:],
        targets,
        sites,
        1.0 / variances,
        begin,
    )

    while local.shape[0] > 1:
        half = local.shape[0] // 2
        pairs = [
            (flat(t, order(t)[i]), flat(t, order(t)[i + half]))
            for t in range(segments)
            for i in range(0, rows, 2 * half)
        ]
        local = local[:half] + lax.ppermute(local[half:], both, pairs)
    own_filtered = local[0, : steps * held].reshape(steps, held * LANES)

    term = jnp.sum(log_jacobian - 0.5 * jnp.log(variances), axis=0, keepdims=True)
    term = term - 0.5 * local[0, steps * held :]
    if segments & (segments - 1):
        term = lax.psum(term, "tm")
    else:
        reach = 1
        while reach < segments:
            term = term + lax.ppermute(term, "tm", [(t, t ^ reach) for t in range(segments)])
            reach *= 2
    count = observations.size * segments
    evidence = jnp.sum(term) / count - 0.5 * math.log(2.0 * math.pi)
    return own_filtered, evidence.reshape(1)


def solution(mesh):
    in_specs = (
        P("tm", None),
        P("tm", None),
        P("tm", None, None),
        P("tm", "row", None, None, None),
        P("tm", "row", None),
        P("tm", None),
        P(),
        P("row"),
    )
    out_specs = (P("tm", "row"), P())
    return jax.shard_map(
        on_device, mesh=mesh, in_specs=in_specs, out_specs=out_specs, check_vma=False
    )
```

```python
import math

import jax
import jax.numpy as jnp
from jax import lax
from jax.experimental import pallas as pl
from jax.experimental.pallas import tpu as pltpu
from jax.sharding import PartitionSpec as P

ORDER = 4
LANES = 128
CHUNKS = (1, 2, 2, 2, 1)
STAGED = 2
VMEM = pl.BlockSpec(memory_space=pltpu.VMEM)
HBM = pl.BlockSpec(memory_space=pltpu.HBM)
SMEM = pl.BlockSpec(memory_space=pltpu.SMEM)


def in_hbm(x):
    return pltpu.with_memory_space_constraint(x, pltpu.HBM)


def split(x):
    high = x.astype(jnp.bfloat16)
    return high, (x - high.astype(jnp.float32)).astype(jnp.bfloat16)


def matmul(a, b):
    return jnp.dot(a, b, preferred_element_type=jnp.float32)


def lane_sums(block):
    return jnp.sum(block.T, axis=0, keepdims=True)


def aligned(row):
    return pl.ds(pl.multiple_of(row * LANES, LANES), LANES)


def compose_kernel(first, last, base, steps, held, nonzero, slots, places, pattern, sites, *refs):
    packs, refs = refs[:slots], refs[slots:]
    targets, refs = refs[0], refs[1:]
    if not first:
        refs = refs[2:]
    high, low, refs = refs[0], refs[1], refs[2:]
    if last:
        whole, refs = refs[0], refs[1:]
    through, seen = refs
    width, columns = high.shape
    pack_rows = held * (nonzero + 1) * LANES
    gain_row = held * nonzero * LANES

    def load(s, t, at):
        start = pl.multiple_of(t * pack_rows + at.start, LANES)
        return packs[s][pl.ds(start, at.size), :]

    def step(t, carry):
        def block_row(s, h):
            row = held * places[s] + h
            picks = [aligned(pattern[base + t, row * nonzero + j]) for j in range(nonzero)]
            if first:
                for j in range(nonzero):
                    block = load(s, t, aligned(h * nonzero + j))
                    through[aligned(row), picks[j]] = through[aligned(row), picks[j]] + block
                return
            parts = [split(load(s, t, aligned(h * nonzero + j))) for j in range(nonzero)]
            up = [p[0] for p in parts]
            down = [p[1] for p in parts]
            tops = [high[pick, :] for pick in picks]
            bottoms = [low[pick, :] for pick in picks]
            through[aligned(row), :] = matmul(
                jnp.concatenate(up + down + up, axis=1),
                jnp.concatenate(tops + tops + bottoms),
            )

        if first:
            through[...] = jnp.zeros_like(through)
        for s in range(slots):
            for h in range(held):
                block_row(s, h)

        def pick_rows(i, carry):
            for u in range(32):
                k = i * 32 + u
                seen[pl.ds(k, 1), :] = through[pl.ds(ORDER * sites[base + t, k], 1), :]
            return carry

        lax.fori_loop(0, LANES // 32, pick_rows, 0)
        target = jnp.broadcast_to(targets[pl.ds(base + t, 1), :], (LANES, LANES)).T
        lane = lax.broadcasted_iota(jnp.int32, (LANES, LANES), 1)
        offset = pl.ds(width, LANES)
        seen[:, offset] = seen[:, offset] - jnp.where(lane == 0, target, 0.0)
        top, bottom = split(seen[...])
        halves = [split(load(s, t, pl.ds(gain_row, held * LANES))) for s in range(slots)]
        left = jnp.concatenate([jnp.concatenate([a, b, a], axis=1) for a, b in halves])
        moved = matmul(left, jnp.concatenate([top, top, bottom]))
        for s in range(slots):
            for h in range(held):
                here = aligned(held * places[s] + h)
                at = (s * held + h) * LANES
                new = through[here, :] - moved[at : at + LANES]
                if last:

                    @pl.when(t == steps - 1)
                    def _(here=here, new=new):
                        whole[here, :] = new

                if not last or steps > 1:
                    a, b = split(new)
                    high[here, :] = a
                    low[here, :] = b
        return carry

    lax.fori_loop(0, steps, step, 0)


def compose(first, last, base, steps, held, nonzero, places, pattern, sites, packs, targets, state):
    slots = len(packs)
    pack_rows = held * (nonzero + 1) * LANES
    width = slots * held * LANES
    columns = width + LANES
    part = jax.ShapeDtypeStruct((width, columns), jnp.bfloat16)
    out_shape = [part, part]
    if last:
        out_shape.append(jax.ShapeDtypeStruct((width, columns), jnp.float32))

    def body(*refs):
        compose_kernel(first, last, base, steps, held, nonzero, slots, *refs)

    done = pl.pallas_call(
        body,
        in_specs=[SMEM] * 3 + [VMEM] * (slots + 1 + len(state)),
        out_specs=[VMEM] * len(out_shape),
        out_shape=out_shape,
        scratch_shapes=[
            pltpu.VMEM((width, columns), jnp.float32),
            pltpu.VMEM((LANES, columns), jnp.float32),
        ],
        cost_estimate=pl.CostEstimate(
            flops=steps * 2 * width * columns * 3 * (nonzero + 1) * LANES,
            transcendentals=0,
            bytes_accessed=4 * slots * steps * pack_rows * LANES,
        ),
        input_output_aliases={} if first else {slots + 4: 0, slots + 5: 1},
        compiler_params=pltpu.CompilerParams(vmem_limit_bytes=36 << 20),
        name="compose",
    )(places, pattern, sites, *packs, targets, *state)
    return done[2] if last else done


def hop_kernel(whole, start, end):
    blocks = start.shape[0]
    for r in range(blocks):
        rows = pl.ds(r * LANES, LANES)
        total = whole[rows, pl.ds(blocks * LANES, LANES)]
        for c in range(blocks):
            total = total + whole[rows, pl.ds(c * LANES, LANES)] * start[pl.ds(c, 1), :]
        end[pl.ds(r, 1), :] = lane_sums(total)


def hop(whole, start):
    return pl.pallas_call(
        hop_kernel,
        in_specs=[VMEM, VMEM],
        out_specs=VMEM,
        out_shape=jax.ShapeDtypeStruct(start.shape, jnp.float32),
        compiler_params=pltpu.CompilerParams(vmem_limit_bytes=2 << 20),
        name="hop",
    )(whole, start)


def fetches(packs, sizes, slots, store, sems):
    rows, steps = store.shape[2], []
    for c, size in enumerate(sizes):
        for i in range(size):
            t = len(steps)
            steps.append(
                [
                    pltpu.make_async_copy(
                        packs[c * slots + s].at[pl.ds(i * rows, rows), :],
                        store.at[s, t],
                        sems.at[s, t],
                    )
                    for s in range(slots)
                ]
            )
    return [copy for step in steps for copy in step]


def stage(sizes, pack_rows, packs, after):
    slots, steps = len(packs[0]), sum(sizes)

    def body(*refs):
        copies = fetches(refs, sizes, slots, refs[-2], refs[-1])
        for copy in copies:
            copy.start()
        for copy in copies:
            copy.wait()

    shape = (slots, steps, pack_rows, LANES)
    return pl.pallas_call(
        body,
        in_specs=[HBM] * (slots * len(sizes)) + [VMEM],
        out_specs=VMEM,
        out_shape=jax.ShapeDtypeStruct(shape, jnp.float32),
        scratch_shapes=[pltpu.SemaphoreType.DMA((slots, steps))],
        cost_estimate=pl.CostEstimate(
            flops=0, transcendentals=0, bytes_accessed=8 * math.prod(shape)
        ),
        compiler_params=pltpu.CompilerParams(vmem_limit_bytes=24 << 20),
        name="stage",
    )(*[in_hbm(p) for pack in packs for p in pack], after)


def segment_kernel(held, nonzero, sizes, slots, places, pattern, owner, store, *refs):
    packs, refs = refs[: slots * len(sizes)], refs[slots * len(sizes) :]
    targets, sites, weights, start, parcels, mean, predicted, rest, sems = refs
    near, far = store.shape[1], rest.shape[1]
    for copy in fetches(packs, sizes, slots, rest, sems):
        copy.start()
    mean[...] = start[...]
    mine = owner[0] == 1

    def step(t, misfit, load):
        innovation = filter_step(
            t, held, nonzero, places, pattern, load, targets, sites, mean, predicted
        )
        for s in range(slots):
            for h in range(held):
                row = mean[pl.ds(held * places[s] + h, 1), :]
                parcels[s, pl.ds(t * held + h, 1), :] = jnp.where(mine, row, 0.0)
        return misfit + innovation * innovation * weights[pl.ds(t, 1), :]

    def near_step(t, misfit):
        return step(t, misfit, lambda s, at: store[s, t, at, :])

    def far_step(t, misfit):
        for s in range(slots):
            rows = pl.ds(0, rest.shape[2])
            pltpu.make_async_copy(packs[s].at[rows, :], rest.at[s, t], sems.at[s, t]).wait()
        return step(near + t, misfit, lambda s, at: rest[s, t, at, :])

    misfit = lax.fori_loop(0, near, near_step, jnp.zeros((1, LANES), jnp.float32))
    misfit = lax.fori_loop(0, far, far_step, misfit)
    for s in range(slots):
        parcels[s, pl.ds((near + far) * held, 1), :] = jnp.where(mine, misfit, 0.0)


def run_segment(
    held, nonzero, sizes, places, pattern, owner, store, packs, targets, sites, weights, start
):
    slots, near, rows = store.shape[:3]
    far = sum(sizes)

    def body(*refs):
        segment_kernel(held, nonzero, sizes, slots, *refs)

    return pl.pallas_call(
        body,
        in_specs=[SMEM] * 3 + [VMEM] + [HBM] * (slots * len(sizes)) + [VMEM] * 4,
        out_specs=VMEM,
        out_shape=jax.ShapeDtypeStruct((slots, (near + far) * held + 1, LANES), jnp.float32),
        scratch_shapes=[
            pltpu.VMEM(start.shape, jnp.float32),
            pltpu.VMEM(start.shape, jnp.float32),
            pltpu.VMEM((slots, far, rows, LANES), jnp.float32),
            pltpu.SemaphoreType.DMA((slots, far)),
        ],
        compiler_params=pltpu.CompilerParams(vmem_limit_bytes=32 << 20),
        name="segment",
    )(
        places,
        pattern,
        owner,
        store,
        *[in_hbm(p) for pack in packs for p in pack],
        targets,
        sites,
        weights,
        start,
    )


def filter_step(t, held, nonzero, places, pattern, load, targets, sites, mean, predicted):
    blocks = mean.shape[0]
    slots = blocks // held
    for s in range(slots):
        for h in range(held):
            row = held * places[s] + h
            total = None
            for j in range(nonzero):
                column = pattern[t, row * nonzero + j]
                block = load(s, pl.ds((h * nonzero + j) * LANES, LANES))
                part = block * mean[pl.ds(column, 1), :]
                total = part if total is None else total + part
            predicted[pl.ds(row, 1), :] = lane_sums(total)
    flat = ORDER * sites[pl.ds(t, 1), :]
    lane = jnp.broadcast_to(flat % LANES, (blocks, LANES))
    picked = jnp.take_along_axis(predicted[...], lane, axis=1)
    block = lax.broadcasted_iota(jnp.int32, (blocks, LANES), 0)
    picked = jnp.where(block == flat // LANES, picked, 0.0)
    innovation = targets[pl.ds(t, 1), :] - jnp.sum(picked, axis=0, keepdims=True)
    for s in range(slots):
        for h in range(held):
            row = held * places[s] + h
            gain = load(s, pl.ds((held * nonzero + h) * LANES, LANES))
            updated = predicted[pl.ds(row, 1), :] + lane_sums(gain * innovation)
            mean[pl.ds(row, 1), :] = updated
    return innovation


def on_device(
    observations,
    sites,
    pattern,
    block_values,
    gains,
    variances,
    monotone_bend_strength,
    initial_mean,
):
    segments, rows = lax.axis_size("tm"), lax.axis_size("row")
    tm, row = lax.axis_index("tm"), lax.axis_index("row")
    steps, held, nonzero = block_values.shape[:3]
    even = tm % 2 == 0

    low = (rows - 1) // 2
    order_even = sorted(range(rows), key=lambda z: (abs(z - low), z))
    order_odd = [rows - 1 - z for z in order_even]

    def order(t):
        return order_even if t % 2 == 0 else order_odd

    def flat(t, z):
        return t * rows + z

    both = ("tm", "row")

    def meet(shard):
        moved = [shard]
        for k in range(1, rows):
            pairs = [(flat(t, order(t)[k]), flat(t, order(t)[0])) for t in range(segments)]
            moved.append(lax.ppermute(shard, both, pairs))
        return moved

    places = jnp.where(
        even, jnp.array(order_even, jnp.int32), jnp.array(order_odd, jnp.int32)
    )
    scale = monotone_bend_strength[0]
    bent = jnp.tanh(observations)
    targets = observations + scale * bent
    log_jacobian = jnp.log(1.0 + scale * (1.0 - bent * bent))
    flat_pattern = pattern.reshape(steps, -1)

    sizes = CHUNKS if sum(CHUNKS) == steps else (1,) * steps
    pack_rows = held * (nonzero + 1) * LANES
    packs, base = [], 0
    for i, size in enumerate(sizes):
        blocks = block_values[base : base + size].reshape(size, -1, LANES)
        pack = jnp.concatenate([blocks, gains[base : base + size]], axis=1)
        pack = pack.reshape(size * pack_rows, LANES)
        if i == 0:
            first = initial_mean.reshape(held, LANES)
            pack = jnp.concatenate([pack, jnp.pad(first, ((0, -held % 8), (0, 0)))])
            pack, block_values, gains = lax.optimization_barrier((pack, block_values, gains))
        packs.append(pack)
        base += size

    packs[:2] = [meet(pack) for pack in packs[:2]]
    state, base = (), 0
    for i, size in enumerate(sizes):
        state = compose(
            i == 0,
            i == len(sizes) - 1,
            base,
            size,
            held,
            nonzero,
            places,
            flat_pattern,
            sites,
            packs[i],
            targets,
            state,
        )
        base += size
        for k in (i + 2, i + 3):
            if k == i + 2 < len(sizes) - 1 or k == i + 3 == len(sizes) - 1:
                packs[k], *state = lax.optimization_barrier((packs[k], *state))
                packs[k] = meet(packs[k])

    starts = [p[sizes[0] * pack_rows :][:held] for p in packs[0]]
    by_even = [starts[order_even.index(z)] for z in range(rows)]
    by_odd = [starts[order_odd.index(z)] for z in range(rows)]
    start = jnp.where(even, jnp.concatenate(by_even), jnp.concatenate(by_odd))

    mean, begin = start, jnp.where(tm == 0, start, 0.0)
    for t in range(segments - 1):
        pair = [(flat(t, order(t)[0]), flat(t + 1, order(t + 1)[0]))]
        ended = hop(state, mean)
        mean = lax.ppermute(ended, both, pair)
        begin = begin + mean
    store = stage(sizes[:STAGED], pack_rows, packs[:STAGED], ended)
    owner = (row == places[:1]).astype(jnp.int32)
    local = run_segment(
        held,
        nonzero,
        sizes[STAGED:],
        places,
        flat_pattern,
        owner,
        store,
        packs[STAGED:],
        targets,
        sites,
        1.0 / variances,
        begin,
    )

    while local.shape[0] > 1:
        half = local.shape[0] // 2
        pairs = [
            (flat(t, order(t)[i]), flat(t, order(t)[i + half]))
            for t in range(segments)
            for i in range(0, rows, 2 * half)
        ]
        local = local[:half] + lax.ppermute(local[half:], both, pairs)
    own_filtered = local[0, : steps * held].reshape(steps, held * LANES)

    term = jnp.sum(log_jacobian - 0.5 * jnp.log(variances), axis=0, keepdims=True)
    term = term - 0.5 * local[0, steps * held :]
    if segments & (segments - 1):
        term = lax.psum(term, "tm")
    else:
        reach = 1
        while reach < segments:
            span = 4 if 4 * reach <= segments else 2
            near = [
                lax.ppermute(term, "tm", [(t, t ^ (k * reach)) for t in range(segments)])
                for k in range(1, span)
            ]
            term = term + near[0]
            if span == 4:
                term = term + (near[1] + near[2])
            reach *= span
    count = observations.size * segments
    evidence = jnp.sum(term) / count - 0.5 * math.log(2.0 * math.pi)
    return own_filtered, evidence.reshape(1)


def solution(mesh):
    in_specs = (
        P("tm", None),
        P("tm", None),
        P("tm", None, None),
        P("tm", "row", None, None, None),
        P("tm", "row", None),
        P("tm", None),
        P(),
        P("row"),
    )
    out_specs = (P("tm", "row"), P())
    return jax.shard_map(
        on_device, mesh=mesh, in_specs=in_specs, out_specs=out_specs, check_vma=False
    )
```
